128 devices in a mesh: row: 8 (over x, z_hi), rhs: 16 (over z_lo, y, core).
Axes of the slice: x: 4, y: 4, z: 4 (z_hi: 2, z_lo: 2; z = z_hi * 2 + z_lo), core: 2. Of those that a mesh axis runs over, the one named last changes fastest.
Arguments:
- right_side: float32 [8, 8, 256, 16384], P(None, 'row', None, 'rhs'), may hold values from -6 to 6
- factor: float32 [8, 8, 256, 1024], P(None, 'row', None, 'rhs'), may hold values from -0.09375 to 0.09375
- inverses: float32 [4, 256, 256], replicated, may hold values from -1 to 2, as said below
- far_operator: float32 [512, 8, 8, 256], P(None, None, 'row'), may hold values from -0.0625 to 0.0625
Outputs:
- solved_rhs: float32 [8, 8, 256, 16384], P(None, 'row', None, 'rhs')
- far_field: float32 [512, 16384], P('row', 'rhs')
The draws below stay inside these ranges and needn't reach their ends.
Inputs may be any that keep to these rules, and one draw needn't show every extreme that they name: inverses of well-conditioned diagonal blocks.
All inputs are finite; a program needn't handle non-finite values.
Results may differ from the reference program's by a relative error of at most 0.0001.
Values sent between devices are 32-bit elements; how exact they have to be, the bound alone decides.
No kernel may reach another device: no remote copies, remote signals or barrier semaphores. Data moves between devices by JAX's collectives and lax.ppermute only.
A program may use at most 128 MiB of HBM per device.

```python
import math
import jax
import jax.numpy as jnp
from jax import lax

BLOCK = 256
PANELS = 4
ANGLES = 512
BLK_DEV = 8
BLOCKS = 64
ROWS = 16384
COLS = 16384
N_ROW = 8


def draw_inverses(key, part):
    base = jnp.eye(BLOCK, dtype=jnp.float32)[None]
    noise = jnp.clip(jax.random.normal(key, (PANELS, BLOCK, BLOCK), jnp.float32), -4.0, 4.0) * (0.6 / math.sqrt(BLOCK))
    return base + noise


def with_spikes(entries, rng, source, target, parts, factor):
    owner, partner = [(jnp.arange(entries.shape[position]) // (entries.shape[position] // parts)).reshape([-1 if axis == position else 1 for axis in range(entries.ndim)]) for position in (source, target)]
    chosen = jax.random.permutation(rng, parts)[partner]
    strong = (owner == chosen) | (owner == (partner + parts // 2) % parts)
    return jnp.where(strong, factor * entries, entries)


def level_of(rng, dims, pieces, smallest, largest):
    loudness, own = 1.0, jax.random.fold_in(rng, 6)
    for axis_at, shards_of in pieces:
        heights = jnp.exp(jax.random.uniform(jax.random.fold_in(own, axis_at), (shards_of,), jnp.float32, smallest / len(pieces), largest / len(pieces)))
        loudness = loudness * jnp.repeat(heights, dims[axis_at] // shards_of).reshape([-1 if axis == axis_at else 1 for axis in range(len(dims))])
    return loudness


def centred(own_key, extent, width, limit, shards=(), held_as=jnp.bfloat16):
    entries = jax.random.normal(own_key, extent, jnp.float32) * width
    if len(shards) > 0:
        entries = level_of(own_key, extent, shards, -0.22, 0.18) * entries
    return jnp.clip(entries, min=-limit, max=limit).astype(held_as)


def noise_with(rng, dims, deviation, bound, split, heavy, held_as=jnp.bfloat16):
    entries = deviation * jax.random.normal(rng, dims, jnp.float32)
    if split:
        entries = entries * level_of(rng, dims, split, -0.22, 0.18)
    return jnp.clip(with_spikes(entries, jax.random.fold_in(rng, 3), *heavy), -bound, bound).astype(held_as)


def setup_inputs(seed: int = 0) -> dict:
    key_list = jax.random.split(jax.random.key(seed), 5)
    return {
        "right_side": centred(key_list[0], (BLK_DEV, N_ROW, BLOCK, COLS), 1.0, 6.0, ((1, 8), (3, 16)), jnp.float32),
        "factor": centred(key_list[1], (BLK_DEV, N_ROW, BLOCK, PANELS * BLOCK), (4 * PANELS * BLOCK) ** -0.5, 0.09375, ((1, 8), (3, 16)), jnp.float32),
        "inverses": draw_inverses(jax.random.fold_in(key_list[4], 71), 0),
        "far_operator": noise_with(key_list[3], (ANGLES, BLK_DEV, N_ROW, BLOCK), ROWS ** -0.5, 0.0625, ((2, 8),), (2, 0, 8, 2.0), jnp.float32),
    }


def product(left_side, right_side):
    return jnp.dot(left_side, right_side, precision=lax.Precision.HIGHEST, preferred_element_type=jnp.float32)


def reference(right_side, factor, inverses, far_operator):
    block_width = BLOCK
    blocks_all = right_side.reshape(BLOCKS, BLOCK, COLS)
    rows_all = factor.reshape(BLOCKS, BLOCK, PANELS * BLOCK)
    solved = []
    for panel_index in range(PANELS):
        current = blocks_all[panel_index]
        for earlier in range(panel_index):
            current = current - product(rows_all[panel_index][:, earlier * block_width:(earlier + 1) * block_width], solved[earlier])
        solved.append(product(inverses[panel_index], current))
    stacked = jnp.concatenate(solved, 0)
    remaining = blocks_all[PANELS:].reshape(-1, COLS) - product(rows_all[PANELS:].reshape(-1, PANELS * BLOCK), stacked)
    flat_rhs = jnp.concatenate([stacked, remaining], 0)
    solved_rhs = flat_rhs.reshape(right_side.shape)
    far_field = product(far_operator.reshape(ANGLES, ROWS), flat_rhs)
    return solved_rhs, far_field
```

```python
import functools

import jax
import jax.numpy as jnp
from jax import lax
from jax.experimental import pallas as pl
from jax.experimental.pallas import tpu as pltpu
from jax.sharding import PartitionSpec as P


F32 = jnp.float32
BF16 = jnp.bfloat16
ROWS, RHS = "row", "rhs"


def row_pairs(move):
    pairs = []
    for x in range(4):
        for high in range(2):
            target = move(x, high)
            if target is not None:
                pairs.append((x * 2 + high, (target[0] % 4) * 2 + target[1]))
    return pairs


def rhs_pairs(move):
    pairs = []
    for low in range(2):
        for y in range(4):
            for core in range(2):
                to = move(low, y, core)
                pairs.append((low * 8 + y * 2 + core, to[0] * 8 + (to[1] % 4) * 2 + to[2]))
    return pairs


CORE = rhs_pairs(lambda low, y, core: (low, y, 1 - core))
HIGH = row_pairs(lambda x, high: (x, 1 - high))
X_UP = row_pairs(lambda x, high: (x + 1, high))
X_DOWN = row_pairs(lambda x, high: (x - 1, high))
X_TWO = row_pairs(lambda x, high: (x + 2, high))
X_PAIR = row_pairs(lambda x, high: (x ^ 1, high))
LEAD_OUT = row_pairs(lambda x, high: (3 - x, high) if x < 2 else None)
LOW = rhs_pairs(lambda low, y, core: (1 - low, y, core))
Y_UP = rhs_pairs(lambda low, y, core: (low, y + 1, core))
Y_DOWN = rhs_pairs(lambda low, y, core: (low, y - 1, core))
Y_ONE = rhs_pairs(lambda low, y, core: (low, y ^ 1, core))
Y_TWO = rhs_pairs(lambda low, y, core: (low, y ^ 2, core))


def halves(value):
    upper = value.astype(BF16)
    return upper, (value - upper.astype(F32)).astype(BF16)


def dot(left, right):
    return jnp.dot(left, right, preferred_element_type=F32)


def triple(left, right_upper, right_lower):
    upper, lower = halves(left)
    return dot(
        jnp.concatenate([upper, lower, upper], 1),
        jnp.concatenate([right_upper, right_upper, right_lower], 0),
    )


def triple_lanes(left, right):
    dims = (((1,), (1,)), ((), ()))
    one = lambda a, b: lax.dot_general(a, b, dims, preferred_element_type=F32)
    upper, lower = halves(left)
    right_upper, right_lower = halves(right)
    return one(upper, right_upper) + one(lower, right_upper) + one(upper, right_lower)


def early_kernel(at, far_ref, rhs_ref, own_ref, out_ref, total):
    step = pl.program_id(0)
    x, high, low, y, core = at[0], at[1], at[2], at[3], at[4]
    angles = total.shape[0]
    per = far_ref.shape[0] // angles
    span = rhs_ref.shape[2]
    width = own_ref.shape[1]
    left = jnp.concatenate(
        [far_ref[pl.ds(2 * step + part, angles, stride=per), :] for part in range(2)], 1
    )
    leads = jnp.logical_and(step == 0, x < 2)
    column = low * 8 + y * 2 + core
    owner = jnp.where(x * 2 + high == column // 4, 1.0, 0.0)
    line = lax.broadcasted_iota(jnp.int32, own_ref.shape[1:], 0) + (column % 4) * width
    lane = lax.broadcasted_iota(jnp.int32, own_ref.shape[1:], 1)
    picked = jnp.where(line == lane, -owner, 0.0)
    own = jnp.where(leads, picked, own_ref[0])
    own = jnp.concatenate([own, jnp.zeros_like(own)], 0)
    through = triple_lanes(left, own)
    left = jnp.where(leads, 0.0, left)
    direct = triple(left, *halves(rhs_ref[0]))

    @pl.when(step == 0)
    def _():
        total[:, :span] = direct
        total[:, span:] = -through

    @pl.when(step > 0)
    def _():
        total[:, :span] += direct
        total[:, span:] -= through

    @pl.when(step == pl.num_programs(0) - 1)
    def _():
        share = out_ref.shape[2]
        for ahead in range(4):
            place = ((x + ahead) % 4) * 2
            for side in range(2):
                turn = high if side == 0 else 1 - high
                out_ref[ahead, side] = total[pl.ds((place + turn) * share, share), :]


def early(at, far_lines, rhs, own, share):
    blocks, height, span = rhs.shape
    width = own.shape[1]
    angles = 8 * share
    lanes = span + 128
    return pl.pallas_call(
        early_kernel,
        out_shape=jax.ShapeDtypeStruct((4, 2, share, lanes), F32),
        grid_spec=pltpu.PrefetchScalarGridSpec(
            num_scalar_prefetch=1,
            grid=(blocks,),
            in_specs=[
                pl.BlockSpec(far_lines.shape, lambda i, s: (0, 0)),
                pl.BlockSpec((1, height, span), lambda i, s: (i, 0, 0)),
                pl.BlockSpec((1, width, height), lambda i, s: (i, 0, 0)),
            ],
            out_specs=pl.BlockSpec((4, 2, share, lanes), lambda i, s: (0, 0, 0, 0)),
            scratch_shapes=[pltpu.VMEM((angles, lanes), F32)],
        ),
        cost_estimate=pl.CostEstimate(
            flops=6 * blocks * angles * height * lanes, bytes_accessed=16 << 20, transcendentals=0
        ),
        name="early",
    )(at, far_lines, rhs, own)


TURNS = (0, 3, 1, 2)
LEAD_SLICES = ((0, 1), (0, 2), (0, 3), (1, 3))
LEAD_AT = 16
HALF = 10


def piece_of(side, turn, index):
    if turn < 3:
        return side * 5 + turn, index
    return side * 5 + 3 + index // HALF, index % HALF


def column_of(at, side, turn, low):
    return low * 8 + ((at[3] + TURNS[turn]) % 4) * 2 + (at[4] + side) % 2


def solve_kernel(at, *refs):
    leads, pieces, refs = refs[:4], refs[4:14], refs[14:]
    inverse_ref, upper_x, lower_x, kept_ref, lead, rows, sems = refs
    x, high = at[0], at[1]
    height = kept_ref.shape[0]
    copies = []

    def fetch(source, into):
        copy = pltpu.make_async_copy(source, into, sems.at[len(copies)])
        copy.start()
        copies.append(copy)

    for pair in range(2):
        near = jnp.where(x < 2, x, 3 - x) if pair == 0 else jnp.where(x < 2, 1 - x, x - 2)
        for side in range(2):
            block = near * 2 + (high if side == 0 else 1 - high)
            fetch(leads[pair * 2 + side], lead.at[pl.ds(block * height, height)])
    for side in range(2):
        for turn in range(4):
            for number, (low, block) in enumerate(LEAD_SLICES):
                piece, index = piece_of(side, turn, LEAD_AT + number)
                fetch(pieces[piece].at[index], rows.at[block - 1, column_of(at, side, turn, low)])
    for copy in copies:
        copy.wait()
    width = rows.shape[2]
    for block in range(4):
        here = pl.ds(block * height, height)
        pending = lead[here, :]
        if block:
            known = block * height
            left = rows[block - 1, : known // width].reshape(known, height).T
            pending = pending - triple(left, upper_x[:known, :], lower_x[:known, :])
        solved = triple(inverse_ref[block], *halves(pending))
        upper, lower = halves(solved)
        upper_x[here, :] = upper
        lower_x[here, :] = lower

        @pl.when(x * 2 + high == block)
        def _():
            kept_ref[...] = solved


def solve(at, leads, pieces, inverses):
    height, span = leads[0].shape
    width = pieces[0].shape[1]
    known = 4 * height
    anywhere = pl.BlockSpec(memory_space=pl.ANY)
    half = jax.ShapeDtypeStruct((known, span), BF16)
    return pl.pallas_call(
        solve_kernel,
        out_shape=(half, half, jax.ShapeDtypeStruct((height, span), F32)),
        grid_spec=pltpu.PrefetchScalarGridSpec(
            num_scalar_prefetch=1,
            grid=(1,),
            in_specs=[anywhere] * 14 + [pl.BlockSpec(inverses.shape, lambda i, s: (0, 0, 0))],
            out_specs=(
                pl.BlockSpec((known, span), lambda i, s: (0, 0)),
                pl.BlockSpec((known, span), lambda i, s: (0, 0)),
                pl.BlockSpec((height, span), lambda i, s: (0, 0)),
            ),
            scratch_shapes=[
                pltpu.VMEM((known, span), F32),
                pltpu.VMEM((3, known // width, width, height), F32),
                pltpu.SemaphoreType.DMA((36,)),
            ],
        ),
        cost_estimate=pl.CostEstimate(
            flops=6 * 10 * height * height * span, bytes_accessed=12 << 20, transcendentals=0
        ),
        name="solve",
    )(at, *leads, *pieces, inverses)


def trail_kernel(start, first, at, *refs):
    pieces, refs = refs[:10], refs[10:]
    upper_x, lower_x, refs = refs[0], refs[1], refs[2:]
    kept_ref, rhs_ref = refs[:2]
    out_ref, panel, sems = refs[-3:]
    step = pl.program_id(0)
    slot = lax.rem(step, 2)

    def fetch(block, slot):
        for side in range(2):
            for turn in range(4):
                for level in range(2):
                    low = (at[2] + level) % 2
                    into = panel.at[slot, column_of(at, side, turn, low)]
                    sem = sems.at[slot, side * 8 + turn * 2 + level]
                    if turn < 3 or level == 0:
                        piece, _ = piece_of(side, turn, 0)
                        source = pieces[piece].at[level * 8 + block]
                        pltpu.make_async_copy(source, into, sem).start()
                    else:
                        piece, cut = piece_of(side, turn, 8)

                        @pl.when(block < HALF - cut)
                        def _():
                            pltpu.make_async_copy(pieces[piece].at[cut + block], into, sem).start()

                        @pl.when(block >= HALF - cut)
                        def _():
                            source = pieces[piece + 1].at[block - (HALF - cut)]
                            pltpu.make_async_copy(source, into, sem).start()

    @pl.when(step == 0)
    def _():
        fetch(start, 0)

    @pl.when(step + 1 < pl.num_programs(0))
    def _():
        fetch(start + step + 1, 1 - slot)

    for number in range(16):
        pltpu.make_async_copy(pieces[0].at[0], panel.at[slot, 0], sems.at[slot, number]).wait()
    known, height = upper_x.shape[0], kept_ref.shape[0]
    left = panel[slot].reshape(known, height).T
    out_ref[0] = rhs_ref[0] - triple(left, upper_x[...], lower_x[...])
    if first:

        @pl.when(jnp.logical_and(step == 0, at[0] < 2))
        def _():
            out_ref[0] = kept_ref[...]


def trail(at, pieces, solved, rhs, start, count, updated):
    _, height, span = rhs.shape
    width = pieces[0].shape[1]
    anywhere = pl.BlockSpec(memory_space=pl.ANY)
    whole = lambda a: pl.BlockSpec(a.shape, lambda i, s: (0,) * a.ndim)
    known = solved[0].shape[0]
    block = pl.BlockSpec((1, height, span), lambda i, s: (start + i, 0, 0))
    before = [] if updated is None else [updated]
    return pl.pallas_call(
        functools.partial(trail_kernel, start, updated is None),
        out_shape=jax.ShapeDtypeStruct(rhs.shape, F32),
        grid_spec=pltpu.PrefetchScalarGridSpec(
            num_scalar_prefetch=1,
            grid=(count,),
            in_specs=[anywhere] * 10 + [whole(a) for a in solved] + [block] + [anywhere] * len(before),
            out_specs=block,
            scratch_shapes=[
                pltpu.VMEM((2, known // width, width, height), F32),
                pltpu.SemaphoreType.DMA((2, 16)),
            ],
        ),
        input_output_aliases={15: 0} if before else {},
        cost_estimate=pl.CostEstimate(
            flops=6 * count * height * known * span, bytes_accessed=count << 22, transcendentals=0
        ),
    )(at, *pieces, *solved, rhs, *before)


def rest_kernel(at, near, far, upper_x, lower_x, a_ref, b_ref, out_ref, turned, sems):
    copies = []
    for side, source in enumerate((near, far)):
        for spot in range(8):
            low = (at[2] + spot // 4) % 2
            column = low * 8 + (at[3] ^ (spot % 4)) * 2 + (at[4] + side) % 2
            copies.append(
                pltpu.make_async_copy(source.at[spot], turned.at[column], sems.at[side * 8 + spot])
            )
    for copy in copies:
        copy.start()
    for copy in copies:
        copy.wait()
    count, _, lanes = turned.shape
    left = [turned[i] + pltpu.roll(turned[i + 1], lanes // 2, axis=1) for i in range(0, count, 2)]
    through = triple(jnp.concatenate(left, 1), upper_x[...], lower_x[...])
    out_ref[...] = a_ref[...] + b_ref[...] + through


def rest(at, near, far, solved, direct, arrived):
    share, lanes = near.shape[1:]
    span = solved[0].shape[1]
    anywhere = pl.BlockSpec(memory_space=pl.ANY)
    whole = pl.BlockSpec(solved[0].shape, lambda i, s: (0, 0))
    part = pl.BlockSpec((share, span), lambda i, s: (0, 0))
    return pl.pallas_call(
        rest_kernel,
        out_shape=jax.ShapeDtypeStruct((share, span), F32),
        grid_spec=pltpu.PrefetchScalarGridSpec(
            num_scalar_prefetch=1,
            grid=(1,),
            in_specs=[anywhere] * 2 + [whole] * 2 + [part] * 2,
            out_specs=part,
            scratch_shapes=[pltpu.VMEM((16, share, lanes), F32), pltpu.SemaphoreType.DMA((16,))],
        ),
        cost_estimate=pl.CostEstimate(
            flops=6 * share * 1024 * span, bytes_accessed=5 << 20, transcendentals=0
        ),
        name="rest",
    )(at, near, far, *solved[:2], direct, arrived)


def step(right_side, factor, inverses, far_operator):
    row, column = lax.axis_index(ROWS), lax.axis_index(RHS)
    x, high = row // 2, row % 2
    low, y, core = column // 8, column // 2 % 4, column % 2
    at = jnp.stack([x, high, low, y, core]).astype(jnp.int32)
    share = far_operator.shape[0] // 8
    rhs = right_side[:, 0]
    span = rhs.shape[2]
    own = jnp.swapaxes(factor[:, 0], 1, 2)
    far_lines = far_operator.reshape(-1, 128)

    slab = own[0]
    slab = jnp.stack([slab, lax.ppermute(slab, RHS, LOW)])
    level = lax.ppermute(own, RHS, LOW)
    near = jnp.where(x < 2, slab, lax.ppermute(slab, ROWS, LEAD_OUT))
    pair = lax.ppermute(near, ROWS, X_PAIR)
    near = jnp.stack([near, pair])
    held = jnp.concatenate([near, lax.ppermute(near, ROWS, HIGH)], 0)
    held = held.reshape(8, *own.shape[1:])
    near_x = jnp.where(x < 2, x, 3 - x)
    slices = [own, level]
    for want_low, block in LEAD_SLICES:
        place = (high != block % 2) * 4 + (near_x != block // 2) * 2 + (low != want_low)
        slices.append(lax.dynamic_index_in_dim(held, place, 0))
    value = jnp.concatenate(slices, 0)

    from_down = lax.ppermute(value, RHS, Y_UP)
    from_up = lax.ppermute(value, RHS, Y_DOWN)
    pieces = [
        value,
        from_down,
        from_up,
        lax.ppermute(from_down[:HALF], RHS, Y_UP),
        lax.ppermute(from_up[HALF:], RHS, Y_DOWN),
    ]
    pieces += [lax.ppermute(value, RHS, CORE) for value in pieces]

    out = lax.ppermute(rhs[0], ROWS, LEAD_OUT)
    first = jnp.where(x < 2, rhs[0], out)
    second = lax.ppermute(first, ROWS, X_PAIR)
    leads = (first, lax.ppermute(first, ROWS, HIGH), second, lax.ppermute(second, ROWS, HIGH))

    sums = early(at, far_lines, rhs, own, share)
    sums = (
        sums[0]
        + lax.ppermute(sums[3], ROWS, X_DOWN)
        + lax.ppermute(sums[1], ROWS, X_UP)
        + lax.ppermute(sums[2], ROWS, X_TWO)
    )
    mine, arrived = sums[0], lax.ppermute(sums[1], ROWS, HIGH)
    through = (mine[:, span:] + arrived[:, span:])[None]
    for pairs in (Y_ONE, Y_TWO, LOW):
        through = jnp.concatenate([through, lax.ppermute(through, RHS, pairs)], 0)
    partner = lax.ppermute(through, RHS, CORE)

    solved = solve(at, leads, pieces, inverses)
    updated = None
    for start, count in ((0, 3), (3, 3), (6, 2)):
        updated = trail(at, pieces, solved, rhs, start, count, updated)
    far_field = rest(at, through, partner, solved, mine, arrived)
    return updated[:, None], far_field


def solution(mesh):
    return jax.shard_map(
        step,
        mesh=mesh,
        in_specs=(
            P(None, "row", None, "rhs"),
            P(None, "row", None, "rhs"),
            P(),
            P(None, None, "row", None),
        ),
        out_specs=(P(None, "row", None, "rhs"), P("row", "rhs")),
        check_vma=False,
    )
```

```python
import jax
import jax.numpy as jnp
from jax import lax
from jax.experimental import pallas as pl
from jax.experimental.pallas import tpu as pltpu
from jax.sharding import PartitionSpec as P


F32 = jnp.float32
BF16 = jnp.bfloat16
ROWS, RHS = "row", "rhs"


def row_pairs(move):
    pairs = []
    for x in range(4):
        for high in range(2):
            target = move(x, high)
            if target is not None:
                pairs.append((x * 2 + high, (target[0] % 4) * 2 + target[1]))
    return pairs


def rhs_pairs(move):
    pairs = []
    for low in range(2):
        for y in range(4):
            for core in range(2):
                to = move(low, y, core)
                pairs.append((low * 8 + y * 2 + core, to[0] * 8 + (to[1] % 4) * 2 + to[2]))
    return pairs


CORE = rhs_pairs(lambda low, y, core: (low, y, 1 - core))
HIGH = row_pairs(lambda x, high: (x, 1 - high))
X_UP = row_pairs(lambda x, high: (x + 1, high))
X_DOWN = row_pairs(lambda x, high: (x - 1, high))
X_TWO = row_pairs(lambda x, high: (x + 2, high))
X_PAIR = row_pairs(lambda x, high: (x ^ 1, high))
LEAD_OUT = row_pairs(lambda x, high: (3 - x, high) if x < 2 else None)
LOW = rhs_pairs(lambda low, y, core: (1 - low, y, core))
Y_UP = rhs_pairs(lambda low, y, core: (low, y + 1, core))
Y_DOWN = rhs_pairs(lambda low, y, core: (low, y - 1, core))
Y_ONE = rhs_pairs(lambda low, y, core: (low, y ^ 1, core))
Y_TWO = rhs_pairs(lambda low, y, core: (low, y ^ 2, core))


def halves(value):
    upper = value.astype(BF16)
    return upper, (value - upper.astype(F32)).astype(BF16)


def dot(left, right):
    return jnp.dot(left, right, preferred_element_type=F32)


def triple(left, right_upper, right_lower):
    upper, lower = halves(left)
    return dot(
        jnp.concatenate([upper, lower, upper], 1),
        jnp.concatenate([right_upper, right_upper, right_lower], 0),
    )


def triple_lanes(left, right):
    dims = (((1,), (1,)), ((), ()))
    one = lambda a, b: lax.dot_general(a, b, dims, preferred_element_type=F32)
    upper, lower = halves(left)
    right_upper, right_lower = halves(right)
    return one(upper, right_upper) + one(lower, right_upper) + one(upper, right_lower)


def far_block(far_ref, step, angles):
    per = far_ref.shape[0] // angles
    return jnp.concatenate(
        [far_ref[pl.ds(2 * step + part, angles, stride=per), :] for part in range(2)], 1
    )


def hand_over(at, total, mine_ref, other_ref):
    share = mine_ref.shape[1]
    for ahead in range(4):
        place = ((at[0] + ahead) % 4) * 2
        mine_ref[ahead] = total[pl.ds((place + at[1]) * share, share), :]
        other_ref[ahead] = total[pl.ds((place + 1 - at[1]) * share, share), :]


def through_kernel(at, far_ref, own_ref, mine_ref, other_ref, total):
    step = pl.program_id(0)
    x, high, low, y, core = at[0], at[1], at[2], at[3], at[4]
    width = own_ref.shape[1]
    left = far_block(far_ref, step, total.shape[0])
    column = low * 8 + y * 2 + core
    owner = jnp.where(x * 2 + high == column // 4, 1.0, 0.0)
    line = lax.broadcasted_iota(jnp.int32, own_ref.shape[1:], 0) + (column % 4) * width
    lane = lax.broadcasted_iota(jnp.int32, own_ref.shape[1:], 1)
    picked = jnp.where(line == lane, -owner, 0.0)
    own = jnp.where(jnp.logical_and(step == 0, x < 2), picked, own_ref[0])
    own = jnp.concatenate([own, jnp.zeros_like(own)], 0)
    through = triple_lanes(left, own)

    @pl.when(step == 0)
    def _():
        total[...] = -through

    @pl.when(step > 0)
    def _():
        total[...] -= through

    @pl.when(step == pl.num_programs(0) - 1)
    def _():
        hand_over(at, total, mine_ref, other_ref)


def early_kernel(at, far_ref, rhs_ref, out_ref, total):
    step = pl.program_id(0)
    left = far_block(far_ref, step, total.shape[0])
    left = jnp.where(jnp.logical_and(step == 0, at[0] < 2), 0.0, left)
    direct = triple(left, *halves(rhs_ref[0]))

    @pl.when(step == 0)
    def _():
        total[...] = direct

    @pl.when(step > 0)
    def _():
        total[...] += direct

    @pl.when(step == pl.num_programs(0) - 1)
    def _():
        share = out_ref.shape[2]
        for ahead in range(4):
            place = ((at[0] + ahead) % 4) * 2
            for side in range(2):
                turn = at[1] if side == 0 else 1 - at[1]
                out_ref[ahead, side] = total[pl.ds((place + turn) * share, share), :]


def far_part(kernel, at, far_lines, operand, share, lanes, joined):
    blocks, depth, span = operand.shape
    angles = 8 * share
    shape = (4, 2, share, lanes) if joined else (4, share, lanes)
    out = [jax.ShapeDtypeStruct(shape, F32)] * (1 if joined else 2)
    whole = pl.BlockSpec(shape, lambda i, s: (0,) * len(shape))
    return pl.pallas_call(
        kernel,
        out_shape=out,
        grid_spec=pltpu.PrefetchScalarGridSpec(
            num_scalar_prefetch=1,
            grid=(blocks,),
            in_specs=[
                pl.BlockSpec(far_lines.shape, lambda i, s: (0, 0)),
                pl.BlockSpec((1, depth, span), lambda i, s: (i, 0, 0)),
            ],
            out_specs=[whole] * len(out),
            scratch_shapes=[pltpu.VMEM((angles, lanes), F32)],
        ),
        cost_estimate=pl.CostEstimate(
            flops=6 * blocks * angles * 256 * lanes, bytes_accessed=12 << 20, transcendentals=0
        ),
    )(at, far_lines, operand)


TURNS = (0, 3, 1, 2)
LEAD_SLICES = ((0, 1), (0, 2), (0, 3), (1, 3))
LEAD_AT = 16
HALF = 10


def piece_of(side, turn, index):
    if turn < 3:
        return side * 5 + turn, index
    return side * 5 + 3 + index // HALF, index % HALF


def column_of(at, side, turn, low):
    return low * 8 + ((at[3] + TURNS[turn]) % 4) * 2 + (at[4] + side) % 2


def pack_kernel(at, own, level, held, out_ref):
    x, high, low = at[0], at[1], at[2]
    near_x = jnp.where(x < 2, x, 3 - x)
    out_ref[:8] = own[...]
    out_ref[8:16] = level[...]
    for number, (want_low, block) in enumerate(LEAD_SLICES):
        place = (
            jnp.where(high != block % 2, 4, 0)
            + jnp.where(near_x != block // 2, 2, 0)
            + jnp.where(low != want_low, 1, 0)
        )
        out_ref[LEAD_AT + number] = held[place]


def pack(at, own, level, held):
    shape = (LEAD_AT + len(LEAD_SLICES), *own.shape[1:])
    whole = lambda shape: pl.BlockSpec(shape, lambda i, s: (0, 0, 0))
    return pl.pallas_call(
        pack_kernel,
        out_shape=jax.ShapeDtypeStruct(shape, F32),
        grid_spec=pltpu.PrefetchScalarGridSpec(
            num_scalar_prefetch=1,
            grid=(1,),
            in_specs=[whole(own.shape), whole(level.shape), whole(held.shape)],
            out_specs=whole(shape),
        ),
        cost_estimate=pl.CostEstimate(flops=0, bytes_accessed=3 << 20, transcendentals=0),
        name="pack",
    )(at, own, level, held)


def late_kernel(at, *refs):
    leads, pieces, through, refs = refs[:4], refs[4:14], refs[14:16], refs[16:]
    inverse_ref, rhs_ref, out_ref, far_ref = refs[:4]
    panel, lead, rows, turned, upper_x, lower_x, kept, panel_sems, sems = refs[4:]
    step = pl.program_id(0)
    slot = lax.rem(step, 2)
    x, high = at[0], at[1]
    height = kept.shape[0]
    known = lead.shape[0]
    width = rows.shape[2]

    def fetch(block, slot):
        for side in range(2):
            for turn in range(4):
                for level in range(2):
                    low = (at[2] + level) % 2
                    into = panel.at[slot, column_of(at, side, turn, low)]
                    sem = panel_sems.at[slot, side * 8 + turn * 2 + level]
                    if turn < 3 or level == 0:
                        piece, _ = piece_of(side, turn, 0)
                        source = pieces[piece].at[level * 8 + block]
                        pltpu.make_async_copy(source, into, sem).start()
                    else:
                        piece, cut = piece_of(side, turn, 8)

                        @pl.when(block < HALF - cut)
                        def _():
                            pltpu.make_async_copy(pieces[piece].at[cut + block], into, sem).start()

                        @pl.when(block >= HALF - cut)
                        def _():
                            source = pieces[piece + 1].at[block - (HALF - cut)]
                            pltpu.make_async_copy(source, into, sem).start()

    @pl.when(step == 0)
    def _():
        copies = []

        def bring(source, into):
            copy = pltpu.make_async_copy(source, into, sems.at[len(copies)])
            copy.start()
            copies.append(copy)

        for pair in range(2):
            near = jnp.where(x < 2, x, 3 - x) if pair == 0 else jnp.where(x < 2, 1 - x, x - 2)
            for side in range(2):
                block = near * 2 + (high if side == 0 else 1 - high)
                bring(leads[pair * 2 + side], lead.at[pl.ds(block * height, height)])
        for side in range(2):
            for turn in range(4):
                for number, (low, block) in enumerate(LEAD_SLICES):
                    piece, index = piece_of(side, turn, LEAD_AT + number)
                    bring(pieces[piece].at[index], rows.at[block - 1, column_of(at, side, turn, low)])
        for side in range(2):
            for spot in range(8):
                low = (at[2] + spot // 4) % 2
                column = low * 8 + (at[3] ^ (spot % 4)) * 2 + (at[4] + side) % 2
                bring(through[side].at[spot], turned.at[column])
        fetch(0, 0)
        for copy in copies:
            copy.wait()
        for block in range(4):
            here = pl.ds(block * height, height)
            pending = lead[here, :]
            if block:
                before = block * height
                left = rows[block - 1, : before // width].reshape(before, height).T
                pending = pending - triple(left, upper_x[:before, :], lower_x[:before, :])
            solved = triple(inverse_ref[block], *halves(pending))
            upper, lower = halves(solved)
            upper_x[here, :] = upper
            lower_x[here, :] = lower

            @pl.when(x * 2 + high == block)
            def _():
                kept[...] = solved

        count, _, lanes = turned.shape
        left = [turned[i] + pltpu.roll(turned[i + 1], lanes // 2, axis=1) for i in range(0, count, 2)]
        far_ref[...] = triple(jnp.concatenate(left, 1), upper_x[...], lower_x[...])

    @pl.when(step + 1 < pl.num_programs(0))
    def _():
        fetch(step + 1, 1 - slot)

    for number in range(16):
        pltpu.make_async_copy(pieces[0].at[0], panel.at[slot, 0], panel_sems.at[slot, number]).wait()
    left = panel[slot].reshape(known, height).T
    out_ref[0] = rhs_ref[0] - triple(left, upper_x[...], lower_x[...])

    @pl.when(jnp.logical_and(step == 0, x < 2))
    def _():
        out_ref[0] = kept[...]


def late(at, leads, pieces, through, inverses, rhs):
    blocks, height, span = rhs.shape
    width = pieces[0].shape[1]
    share, lanes = through[0].shape[1:]
    known = 4 * height
    anywhere = pl.BlockSpec(memory_space=pl.ANY)
    block = pl.BlockSpec((1, height, span), lambda i, s: (i, 0, 0))
    return pl.pallas_call(
        late_kernel,
        out_shape=(
            jax.ShapeDtypeStruct(rhs.shape, F32),
            jax.ShapeDtypeStruct((share, span), F32),
        ),
        grid_spec=pltpu.PrefetchScalarGridSpec(
            num_scalar_prefetch=1,
            grid=(blocks,),
            in_specs=[anywhere] * 16 + [pl.BlockSpec(inverses.shape, lambda i, s: (0, 0, 0)), block],
            out_specs=(block, pl.BlockSpec((share, span), lambda i, s: (0, 0))),
            scratch_shapes=[
                pltpu.VMEM((2, known // width, width, height), F32),
                pltpu.VMEM((known, span), F32),
                pltpu.VMEM((3, known // width, width, height), F32),
                pltpu.VMEM((16, share, lanes), F32),
                pltpu.VMEM((known, span), BF16),
                pltpu.VMEM((known, span), BF16),
                pltpu.VMEM((height, span), F32),
                pltpu.SemaphoreType.DMA((2, 16)),
                pltpu.SemaphoreType.DMA((52,)),
            ],
        ),
        cost_estimate=pl.CostEstimate(
            flops=6 * blocks * height * known * span, bytes_accessed=32 << 20, transcendentals=0
        ),
        name="late",
    )(at, *leads, *pieces, *through, inverses, rhs)


def step(right_side, factor, inverses, far_operator):
    row, column = lax.axis_index(ROWS), lax.axis_index(RHS)
    x, high = row // 2, row % 2
    low, y, core = column // 8, column // 2 % 4, column % 2
    at = jnp.stack([x, high, low, y, core]).astype(jnp.int32)
    share = far_operator.shape[0] // 8
    rhs = right_side[:, 0]
    span = rhs.shape[2]
    own = jnp.swapaxes(factor[:, 0], 1, 2)
    far_lines = far_operator.reshape(-1, 128)

    slab = own[0]
    slab = jnp.stack([slab, lax.ppermute(slab, RHS, LOW)])
    level = lax.ppermute(own, RHS, LOW)
    near = jnp.where(x < 2, slab, lax.ppermute(slab, ROWS, LEAD_OUT))
    pair = lax.ppermute(near, ROWS, X_PAIR)
    near = jnp.stack([near, pair])
    held = jnp.concatenate([near, lax.ppermute(near, ROWS, HIGH)], 0)
    value = pack(at, own, level, held.reshape(8, *own.shape[1:]))

    from_down = lax.ppermute(value, RHS, Y_UP)
    from_up = lax.ppermute(value, RHS, Y_DOWN)
    pieces = [
        value,
        from_down,
        from_up,
        lax.ppermute(from_down[:HALF], RHS, Y_UP),
        lax.ppermute(from_up[HALF:], RHS, Y_DOWN),
    ]
    pieces += [lax.ppermute(value, RHS, CORE) for value in pieces]

    out = lax.ppermute(rhs[0], ROWS, LEAD_OUT)
    first = jnp.where(x < 2, rhs[0], out)
    second = lax.ppermute(first, ROWS, X_PAIR)
    leads = (first, lax.ppermute(first, ROWS, HIGH), second, lax.ppermute(second, ROWS, HIGH))

    mine, other = far_part(through_kernel, at, far_lines, own, share, 128, False)
    mine = mine + lax.ppermute(other, ROWS, HIGH)
    through = (
        mine[0]
        + lax.ppermute(mine[3], ROWS, X_DOWN)
        + lax.ppermute(mine[1], ROWS, X_UP)
        + lax.ppermute(mine[2], ROWS, X_TWO)
    )[None]
    for pairs in (Y_ONE, Y_TWO, LOW):
        through = jnp.concatenate([through, lax.ppermute(through, RHS, pairs)], 0)
    through = (through, lax.ppermute(through, RHS, CORE))

    (sums,) = far_part(early_kernel, at, far_lines, rhs, share, span, True)
    sums = (
        sums[0]
        + lax.ppermute(sums[3], ROWS, X_DOWN)
        + lax.ppermute(sums[1], ROWS, X_UP)
        + lax.ppermute(sums[2], ROWS, X_TWO)
    )
    direct = sums[0] + lax.ppermute(sums[1], ROWS, HIGH)

    solved, rest = late(at, leads, pieces, through, inverses, rhs)
    return solved[:, None], direct + rest


def solution(mesh):
    return jax.shard_map(
        step,
        mesh=mesh,
        in_specs=(
            P(None, "row", None, "rhs"),
            P(None, "row", None, "rhs"),
            P(),
            P(None, None, "row", None),
        ),
        out_specs=(P(None, "row", None, "rhs"), P("row", "rhs")),
        check_vma=False,
    )
```

```python
import jax
import jax.numpy as jnp
from jax import lax
from jax.experimental import pallas as pl
from jax.experimental.pallas import tpu as pltpu
from jax.sharding import PartitionSpec as P


F32 = jnp.float32
BF16 = jnp.bfloat16
ROWS, RHS = "row", "rhs"


def row_pairs(move):
    pairs = []
    for x in range(4):
        for high in range(2):
            target = move(x, high)
            if target is not None:
                pairs.append((x * 2 + high, (target[0] % 4) * 2 + target[1]))
    return pairs


def rhs_pairs(move):
    pairs = []
    for low in range(2):
        for y in range(4):
            for core in range(2):
                to = move(low, y, core)
                pairs.append((low * 8 + y * 2 + core, to[0] * 8 + (to[1] % 4) * 2 + to[2]))
    return pairs


CORE = rhs_pairs(lambda low, y, core: (low, y, 1 - core))
HIGH = row_pairs(lambda x, high: (x, 1 - high))
X_UP = row_pairs(lambda x, high: (x + 1, high))
X_DOWN = row_pairs(lambda x, high: (x - 1, high))
X_TWO = row_pairs(lambda x, high: (x + 2, high))
X_PAIR = row_pairs(lambda x, high: (x ^ 1, high))
LEAD_OUT = row_pairs(lambda x, high: (3 - x, high) if x < 2 else None)
LOW = rhs_pairs(lambda low, y, core: (1 - low, y, core))
Y_UP = rhs_pairs(lambda low, y, core: (low, y + 1, core))
Y_DOWN = rhs_pairs(lambda low, y, core: (low, y - 1, core))


def halves(value):
    upper = value.astype(BF16)
    return upper, (value - upper.astype(F32)).astype(BF16)


def dot(left, right):
    return jnp.dot(left, right, preferred_element_type=F32)


def triple(left, right_upper, right_lower):
    upper, lower = halves(left)
    return dot(
        jnp.concatenate([upper, lower, upper], 1),
        jnp.concatenate([right_upper, right_upper, right_lower], 0),
    )


def triple_lanes(left, right):
    dims = (((1,), (1,)), ((), ()))
    one = lambda a, b: lax.dot_general(a, b, dims, preferred_element_type=F32)
    upper, lower = halves(left)
    right_upper, right_lower = halves(right)
    return one(upper, right_upper) + one(lower, right_upper) + one(upper, right_lower)


def hand_over(at, total, out_ref):
    share = out_ref.shape[2]
    for ahead in range(4):
        place = ((at[0] + ahead) % 4) * 2
        for side in range(2):
            turn = at[1] if side == 0 else 1 - at[1]
            out_ref[ahead, side] = total[pl.ds((place + turn) * share, share), :]


def far_block(far_ref, far, sems):
    step = pl.program_id(0)
    parts = far.shape[0] // pl.num_programs(0)

    def copy(part):
        return pltpu.make_async_copy(far_ref.at[:, part], far.at[part], sems.at[part])

    @pl.when(step == 0)
    def _():
        for part in range(far.shape[0]):
            copy(part).start()

    for part in range(parts):
        copy(step * parts + part).wait()
    return jnp.concatenate([far[step * parts + part] for part in range(parts)], 1)


def through_kernel(at, far_ref, own_ref, out_ref, total, far, sems):
    step = pl.program_id(0)
    x, high, low, y, core = at[0], at[1], at[2], at[3], at[4]
    width = own_ref.shape[1]
    left = far_block(far_ref, far, sems)
    column = low * 8 + y * 2 + core
    owner = jnp.where(x * 2 + high == column // 4, 1.0, 0.0)
    line = lax.broadcasted_iota(jnp.int32, own_ref.shape[1:], 0) + (column % 4) * width
    lane = lax.broadcasted_iota(jnp.int32, own_ref.shape[1:], 1)
    picked = jnp.where(line == lane, -owner, 0.0)
    own = jnp.where(jnp.logical_and(step == 0, x < 2), picked, own_ref[0])
    own = jnp.concatenate([own, jnp.zeros_like(own)], 0)
    through = triple_lanes(left, own)

    @pl.when(step == 0)
    def _():
        total[...] = -through

    @pl.when(step > 0)
    def _():
        total[...] -= through

    @pl.when(step == pl.num_programs(0) - 1)
    def _():
        hand_over(at, total, out_ref)


def early_kernel(at, far_ref, rhs_ref, out_ref, total, far, sems):
    step = pl.program_id(0)
    left = far_block(far_ref, far, sems)
    left = jnp.where(jnp.logical_and(step == 0, at[0] < 2), 0.0, left)
    direct = triple(left, *halves(rhs_ref[0]))

    @pl.when(step == 0)
    def _():
        total[...] = direct

    @pl.when(step > 0)
    def _():
        total[...] += direct

    @pl.when(step == pl.num_programs(0) - 1)
    def _():
        hand_over(at, total, out_ref)


def far_part(kernel, at, far_lines, operand, share, lanes):
    blocks, depth, span = operand.shape
    angles, parts, line = far_lines.shape
    shape = (4, 2, share, lanes)
    return pl.pallas_call(
        kernel,
        out_shape=jax.ShapeDtypeStruct(shape, F32),
        grid_spec=pltpu.PrefetchScalarGridSpec(
            num_scalar_prefetch=1,
            grid=(blocks,),
            in_specs=[
                pl.BlockSpec(memory_space=pl.ANY),
                pl.BlockSpec((1, depth, span), lambda i, s: (i, 0, 0)),
            ],
            out_specs=pl.BlockSpec(shape, lambda i, s: (0, 0, 0, 0)),
            scratch_shapes=[
                pltpu.VMEM((angles, lanes), F32),
                pltpu.VMEM((parts, angles, line), F32),
                pltpu.SemaphoreType.DMA((parts,)),
            ],
        ),
        cost_estimate=pl.CostEstimate(
            flops=6 * blocks * angles * 256 * lanes, bytes_accessed=12 << 20, transcendentals=0
        ),
    )(at, far_lines, operand)


TURNS = (0, 3, 1, 2)
LEAD_SLICES = ((0, 1), (0, 2), (0, 3), (1, 3))
LEAD_AT = 16
THROUGH_AT = 20
HALF = 11


def piece_of(side, turn, index):
    if turn < 3:
        return side * 5 + turn, index
    return side * 5 + 3 + index // HALF, index % HALF


def column_of(at, side, turn, low):
    return low * 8 + ((at[3] + TURNS[turn]) % 4) * 2 + (at[4] + side) % 2


def pack_kernel(at, own, level, held, near, far, out_ref):
    x, high, low = at[0], at[1], at[2]
    near_x = jnp.where(x < 2, x, 3 - x)
    out_ref[:8] = own[...]
    out_ref[8:16] = level[...]
    for number, (want_low, block) in enumerate(LEAD_SLICES):
        place = (
            jnp.where(high != block % 2, 4, 0)
            + jnp.where(near_x != block // 2, 2, 0)
            + jnp.where(low != want_low, 1, 0)
        )
        out_ref[LEAD_AT + number] = held[place]
    lanes = near.shape[1]
    out_ref[THROUGH_AT, :, :lanes] = near[...]
    out_ref[THROUGH_AT, :, lanes:] = far[...]


def pack(at, *operands):
    shape = (THROUGH_AT + 1, *operands[0].shape[1:])
    whole = lambda shape: pl.BlockSpec(shape, lambda i, s: (0,) * len(shape))
    return pl.pallas_call(
        pack_kernel,
        out_shape=jax.ShapeDtypeStruct(shape, F32),
        grid_spec=pltpu.PrefetchScalarGridSpec(
            num_scalar_prefetch=1,
            grid=(1,),
            in_specs=[whole(a.shape) for a in operands],
            out_specs=whole(shape),
        ),
        cost_estimate=pl.CostEstimate(flops=0, bytes_accessed=3 << 20, transcendentals=0),
        name="pack",
    )(at, *operands)


def late_kernel(at, *refs):
    leads, pieces, refs = refs[:4], refs[4:14], refs[14:]
    inverse_ref, rhs_ref, out_ref, far_ref = refs[:4]
    panel, lead, rows, turned, upper_x, lower_x, kept, panel_sems, sems = refs[4:]
    step = pl.program_id(0)
    slot = lax.rem(step, 2)
    x, high = at[0], at[1]
    height = kept.shape[0]
    known = lead.shape[0]
    width = rows.shape[2]

    def fetch(block, slot):
        for side in range(2):
            for turn in range(4):
                for level in range(2):
                    low = (at[2] + level) % 2
                    into = panel.at[slot, column_of(at, side, turn, low)]
                    sem = panel_sems.at[slot, side * 8 + turn * 2 + level]
                    if turn < 3 or level == 0:
                        piece, _ = piece_of(side, turn, 0)
                        source = pieces[piece].at[level * 8 + block]
                        pltpu.make_async_copy(source, into, sem).start()
                    else:
                        piece, cut = piece_of(side, turn, 8)

                        @pl.when(block < HALF - cut)
                        def _():
                            pltpu.make_async_copy(pieces[piece].at[cut + block], into, sem).start()

                        @pl.when(block >= HALF - cut)
                        def _():
                            source = pieces[piece + 1].at[block - (HALF - cut)]
                            pltpu.make_async_copy(source, into, sem).start()

    @pl.when(step == 0)
    def _():
        copies = []

        def bring(source, into):
            copy = pltpu.make_async_copy(source, into, sems.at[len(copies)])
            copy.start()
            copies.append(copy)

        for pair in range(2):
            near = jnp.where(x < 2, x, 3 - x) if pair == 0 else jnp.where(x < 2, 1 - x, x - 2)
            for side in range(2):
                block = near * 2 + (high if side == 0 else 1 - high)
                bring(leads[pair * 2 + side], lead.at[pl.ds(block * height, height)])
        for side in range(2):
            for turn in range(4):
                for number, (low, block) in enumerate(LEAD_SLICES):
                    piece, index = piece_of(side, turn, LEAD_AT + number)
                    bring(pieces[piece].at[index], rows.at[block - 1, column_of(at, side, turn, low)])
        lanes = turned.shape[2]
        for side in range(2):
            for turn in range(4):
                for level in range(2):
                    piece, index = piece_of(side, turn, THROUGH_AT)
                    source = pieces[piece].at[index, :, pl.ds(level * lanes, lanes)]
                    bring(source, turned.at[column_of(at, side, turn, (at[2] + level) % 2)])
        fetch(0, 0)
        for copy in copies:
            copy.wait()
        for block in range(4):
            here = pl.ds(block * height, height)
            pending = lead[here, :]
            if block:
                before = block * height
                left = rows[block - 1, : before // width].reshape(before, height).T
                pending = pending - triple(left, upper_x[:before, :], lower_x[:before, :])
            solved = triple(inverse_ref[block], *halves(pending))
            upper, lower = halves(solved)
            upper_x[here, :] = upper
            lower_x[here, :] = lower

            @pl.when(x * 2 + high == block)
            def _():
                kept[...] = solved

        count = turned.shape[0]
        left = [turned[i] + pltpu.roll(turned[i + 1], lanes // 2, axis=1) for i in range(0, count, 2)]
        far_ref[...] = triple(jnp.concatenate(left, 1), upper_x[...], lower_x[...])

    @pl.when(step + 1 < pl.num_programs(0))
    def _():
        fetch(step + 1, 1 - slot)

    for number in range(16):
        pltpu.make_async_copy(pieces[0].at[0], panel.at[slot, 0], panel_sems.at[slot, number]).wait()
    left = panel[slot].reshape(known, height).T
    out_ref[0] = rhs_ref[0] - triple(left, upper_x[...], lower_x[...])

    @pl.when(jnp.logical_and(step == 0, x < 2))
    def _():
        out_ref[0] = kept[...]


def late(at, leads, pieces, share, inverses, rhs):
    blocks, height, span = rhs.shape
    width = pieces[0].shape[1]
    lanes = pieces[0].shape[2] // 2
    known = 4 * height
    anywhere = pl.BlockSpec(memory_space=pl.ANY)
    block = pl.BlockSpec((1, height, span), lambda i, s: (i, 0, 0))
    return pl.pallas_call(
        late_kernel,
        out_shape=(
            jax.ShapeDtypeStruct(rhs.shape, F32),
            jax.ShapeDtypeStruct((share, span), F32),
        ),
        grid_spec=pltpu.PrefetchScalarGridSpec(
            num_scalar_prefetch=1,
            grid=(blocks,),
            in_specs=[anywhere] * 14 + [pl.BlockSpec(inverses.shape, lambda i, s: (0, 0, 0)), block],
            out_specs=(block, pl.BlockSpec((share, span), lambda i, s: (0, 0))),
            scratch_shapes=[
                pltpu.VMEM((2, known // width, width, height), F32),
                pltpu.VMEM((known, span), F32),
                pltpu.VMEM((3, known // width, width, height), F32),
                pltpu.VMEM((16, share, lanes), F32),
                pltpu.VMEM((known, span), BF16),
                pltpu.VMEM((known, span), BF16),
                pltpu.VMEM((height, span), F32),
                pltpu.SemaphoreType.DMA((2, 16)),
                pltpu.SemaphoreType.DMA((52,)),
            ],
        ),
        cost_estimate=pl.CostEstimate(
            flops=6 * blocks * height * known * span, bytes_accessed=32 << 20, transcendentals=0
        ),
        name="late",
    )(at, *leads, *pieces, inverses, rhs)


def summed(sums):
    sums = (
        sums[0]
        + lax.ppermute(sums[3], ROWS, X_DOWN)
        + lax.ppermute(sums[1], ROWS, X_UP)
        + lax.ppermute(sums[2], ROWS, X_TWO)
    )
    return sums[0] + lax.ppermute(sums[1], ROWS, HIGH)


def step(right_side, factor, inverses, far_operator):
    row, column = lax.axis_index(ROWS), lax.axis_index(RHS)
    x, high = row // 2, row % 2
    low, y, core = column // 8, column // 2 % 4, column % 2
    at = jnp.stack([x, high, low, y, core]).astype(jnp.int32)
    share = far_operator.shape[0] // 8
    rhs = right_side[:, 0]
    span = rhs.shape[2]
    own = jnp.swapaxes(factor[:, 0], 1, 2)
    far_lines = far_operator.reshape(far_operator.shape[0], -1, 128)

    slab = own[0]
    slab = jnp.stack([slab, lax.ppermute(slab, RHS, LOW)])
    level = lax.ppermute(own, RHS, LOW)
    near = jnp.where(x < 2, slab, lax.ppermute(slab, ROWS, LEAD_OUT))
    pair = lax.ppermute(near, ROWS, X_PAIR)
    near = jnp.stack([near, pair])
    held = jnp.concatenate([near, lax.ppermute(near, ROWS, HIGH)], 0)
    held = held.reshape(8, *own.shape[1:])

    sums = far_part(through_kernel, at, far_lines, own, share, 128)
    through = summed(sums)

    value = pack(at, own, level, held, through, lax.ppermute(through, RHS, LOW))

    from_down = lax.ppermute(value, RHS, Y_UP)
    from_up = lax.ppermute(value, RHS, Y_DOWN)
    pieces = [
        value,
        from_down,
        from_up,
        lax.ppermute(from_down[:HALF], RHS, Y_UP),
        lax.ppermute(from_up[HALF:], RHS, Y_DOWN),
    ]
    pieces += [lax.ppermute(value, RHS, CORE) for value in pieces]

    out = lax.ppermute(rhs[0], ROWS, LEAD_OUT)
    first = jnp.where(x < 2, rhs[0], out)
    second = lax.ppermute(first, ROWS, X_PAIR)
    leads = (first, lax.ppermute(first, ROWS, HIGH), second, lax.ppermute(second, ROWS, HIGH))

    sums = far_part(early_kernel, at, far_lines, rhs, share, span)
    direct = summed(sums)

    solved, rest = late(at, leads, pieces, share, inverses, rhs)
    return solved[:, None], direct + rest


def solution(mesh):
    return jax.shard_map(
        step,
        mesh=mesh,
        in_specs=(
            P(None, "row", None, "rhs"),
            P(None, "row", None, "rhs"),
            P(),
            P(None, None, "row", None),
        ),
        out_specs=(P(None, "row", None, "rhs"), P("row", "rhs")),
        check_vma=False,
    )
```

```python
import jax
import jax.numpy as jnp
from jax import lax
from jax.experimental import pallas as pl
from jax.experimental.pallas import tpu as pltpu
from jax.sharding import PartitionSpec as P


F32 = jnp.float32
BF16 = jnp.bfloat16
ROWS, RHS = "row", "rhs"


def row_pairs(move):
    pairs = []
    for x in range(4):
        for high in range(2):
            target = move(x, high)
            if target is not None:
                pairs.append((x * 2 + high, (target[0] % 4) * 2 + target[1]))
    return pairs


def rhs_pairs(move):
    pairs = []
    for low in range(2):
        for y in range(4):
            for core in range(2):
                to = move(low, y, core)
                pairs.append((low * 8 + y * 2 + core, to[0] * 8 + (to[1] % 4) * 2 + to[2]))
    return pairs


CORE = rhs_pairs(lambda low, y, core: (low, y, 1 - core))
HIGH = row_pairs(lambda x, high: (x, 1 - high))
X_UP = row_pairs(lambda x, high: (x + 1, high))
X_DOWN = row_pairs(lambda x, high: (x - 1, high))
X_TWO = row_pairs(lambda x, high: (x + 2, high))
X_PAIR = row_pairs(lambda x, high: (x ^ 1, high))
LEAD_OUT = row_pairs(lambda x, high: (3 - x, high) if x < 2 else None)
LOW = rhs_pairs(lambda low, y, core: (1 - low, y, core))
Y_UP = rhs_pairs(lambda low, y, core: (low, y + 1, core))
Y_DOWN = rhs_pairs(lambda low, y, core: (low, y - 1, core))


def halves(value):
    upper = value.astype(BF16)
    return upper, (value - upper.astype(F32)).astype(BF16)


def dot(left, right):
    return jnp.dot(left, right, preferred_element_type=F32)


def triple(left, right_upper, right_lower):
    upper, lower = halves(left)
    return dot(
        jnp.concatenate([upper, lower, upper], 1),
        jnp.concatenate([right_upper, right_upper, right_lower], 0),
    )


def triple_lanes(left, right):
    dims = (((1,), (1,)), ((), ()))
    one = lambda a, b: lax.dot_general(a, b, dims, preferred_element_type=F32)
    upper, lower = halves(left)
    right_upper, right_lower = halves(right)
    return one(upper, right_upper) + one(lower, right_upper) + one(upper, right_lower)


def hand_over(at, total, outs):
    share = outs[0].shape[1]
    for ahead, out_ref in enumerate(outs):
        place = ((at[0] + ahead) % 4) * 2
        for side in range(2):
            turn = at[1] if side == 0 else 1 - at[1]
            out_ref[side] = total[pl.ds((place + turn) * share, share), :]


def far_block(far_ref, far, sems):
    step = pl.program_id(0)
    parts = far.shape[0] // pl.num_programs(0)

    def copy(part):
        return pltpu.make_async_copy(far_ref.at[:, part], far.at[part], sems.at[part])

    @pl.when(step == 0)
    def _():
        for part in range(far.shape[0]):
            copy(part).start()

    for part in range(parts):
        copy(step * parts + part).wait()
    return jnp.concatenate([far[step * parts + part] for part in range(parts)], 1)


def through_kernel(at, far_ref, own_ref, *refs):
    outs, (total, far, sems) = refs[:4], refs[4:]
    step = pl.program_id(0)
    x, high, low, y, core = at[0], at[1], at[2], at[3], at[4]
    width = own_ref.shape[1]
    left = far_block(far_ref, far, sems)
    column = low * 8 + y * 2 + core
    owner = jnp.where(x * 2 + high == column // 4, 1.0, 0.0)
    line = lax.broadcasted_iota(jnp.int32, own_ref.shape[1:], 0) + (column % 4) * width
    lane = lax.broadcasted_iota(jnp.int32, own_ref.shape[1:], 1)
    picked = jnp.where(line == lane, -owner, 0.0)
    own = jnp.where(jnp.logical_and(step == 0, x < 2), picked, own_ref[0])
    own = jnp.concatenate([own, jnp.zeros_like(own)], 0)
    through = triple_lanes(left, own)

    @pl.when(step == 0)
    def _():
        total[...] = -through

    @pl.when(step > 0)
    def _():
        total[...] -= through

    @pl.when(step == pl.num_programs(0) - 1)
    def _():
        hand_over(at, total, outs)


def early_kernel(at, far_ref, rhs_ref, *refs):
    outs, (total, far, sems) = refs[:4], refs[4:]
    step = pl.program_id(0)
    left = far_block(far_ref, far, sems)
    left = jnp.where(jnp.logical_and(step == 0, at[0] < 2), 0.0, left)
    direct = triple(left, *halves(rhs_ref[0]))

    @pl.when(step == 0)
    def _():
        total[...] = direct

    @pl.when(step > 0)
    def _():
        total[...] += direct

    @pl.when(step == pl.num_programs(0) - 1)
    def _():
        hand_over(at, total, outs)


def far_part(kernel, at, far_lines, operand, share, lanes):
    blocks, depth, span = operand.shape
    angles, parts, line = far_lines.shape
    shape = (2, share, lanes)
    return pl.pallas_call(
        kernel,
        out_shape=[jax.ShapeDtypeStruct(shape, F32)] * 4,
        grid_spec=pltpu.PrefetchScalarGridSpec(
            num_scalar_prefetch=1,
            grid=(blocks,),
            in_specs=[
                pl.BlockSpec(memory_space=pl.ANY),
                pl.BlockSpec((1, depth, span), lambda i, s: (i, 0, 0)),
            ],
            out_specs=[pl.BlockSpec(shape, lambda i, s: (0, 0, 0))] * 4,
            scratch_shapes=[
                pltpu.VMEM((angles, lanes), F32),
                pltpu.VMEM((parts, angles, line), F32),
                pltpu.SemaphoreType.DMA((parts,)),
            ],
        ),
        cost_estimate=pl.CostEstimate(
            flops=6 * blocks * angles * 256 * lanes, bytes_accessed=12 << 20, transcendentals=0
        ),
    )(at, far_lines, operand)


TURNS = (0, 3, 1, 2)
LEAD_SLICES = ((0, 1), (0, 2), (0, 3), (1, 3))
LEAD_AT = 16
THROUGH_AT = 20
HALF = 11


def piece_of(side, turn, index):
    if turn < 3:
        return side * 5 + turn, index
    return side * 5 + 3 + index // HALF, index % HALF


def column_of(at, side, turn, low):
    return low * 8 + ((at[3] + TURNS[turn]) % 4) * 2 + (at[4] + side) % 2


def pack_kernel(at, own, level, held, near, far, out_ref):
    x, high, low = at[0], at[1], at[2]
    near_x = jnp.where(x < 2, x, 3 - x)
    out_ref[:8] = own[...]
    out_ref[8:16] = level[...]
    for number, (want_low, block) in enumerate(LEAD_SLICES):
        place = (
            jnp.where(high != block % 2, 4, 0)
            + jnp.where(near_x != block // 2, 2, 0)
            + jnp.where(low != want_low, 1, 0)
        )
        out_ref[LEAD_AT + number] = held[place]
    lanes = near.shape[1]
    out_ref[THROUGH_AT, :, :lanes] = near[...]
    out_ref[THROUGH_AT, :, lanes:] = far[...]


def pack(at, *operands):
    shape = (THROUGH_AT + 1, *operands[0].shape[1:])
    whole = lambda shape: pl.BlockSpec(shape, lambda i, s: (0,) * len(shape))
    return pl.pallas_call(
        pack_kernel,
        out_shape=jax.ShapeDtypeStruct(shape, F32),
        grid_spec=pltpu.PrefetchScalarGridSpec(
            num_scalar_prefetch=1,
            grid=(1,),
            in_specs=[whole(a.shape) for a in operands],
            out_specs=whole(shape),
        ),
        cost_estimate=pl.CostEstimate(flops=0, bytes_accessed=3 << 20, transcendentals=0),
        name="pack",
    )(at, *operands)


def late_kernel(at, *refs):
    leads, pieces, refs = refs[:4], refs[4:14], refs[14:]
    inverse_ref, rhs_ref, out_ref, far_ref = refs[:4]
    panel, lead, rows, turned, upper_x, lower_x, kept, panel_sems, sems = refs[4:]
    step = pl.program_id(0)
    slot = lax.rem(step, 2)
    x, high = at[0], at[1]
    height = kept.shape[0]
    known = lead.shape[0]
    width = rows.shape[2]

    def fetch(block, slot):
        for side in range(2):
            for turn in range(4):
                for level in range(2):
                    low = (at[2] + level) % 2
                    into = panel.at[slot, column_of(at, side, turn, low)]
                    sem = panel_sems.at[slot, side * 8 + turn * 2 + level]
                    if turn < 3 or level == 0:
                        piece, _ = piece_of(side, turn, 0)
                        source = pieces[piece].at[level * 8 + block]
                        pltpu.make_async_copy(source, into, sem).start()
                    else:
                        piece, cut = piece_of(side, turn, 8)

                        @pl.when(block < HALF - cut)
                        def _():
                            pltpu.make_async_copy(pieces[piece].at[cut + block], into, sem).start()

                        @pl.when(block >= HALF - cut)
                        def _():
                            source = pieces[piece + 1].at[block - (HALF - cut)]
                            pltpu.make_async_copy(source, into, sem).start()

    @pl.when(step == 0)
    def _():
        copies = []

        def bring(source, into):
            copy = pltpu.make_async_copy(source, into, sems.at[len(copies)])
            copy.start()
            copies.append(copy)

        for pair in range(2):
            near = jnp.where(x < 2, x, 3 - x) if pair == 0 else jnp.where(x < 2, 1 - x, x - 2)
            for side in range(2):
                block = near * 2 + (high if side == 0 else 1 - high)
                bring(leads[pair * 2 + side], lead.at[pl.ds(block * height, height)])
        for side in range(2):
            for turn in range(4):
                for number, (low, block) in enumerate(LEAD_SLICES):
                    piece, index = piece_of(side, turn, LEAD_AT + number)
                    bring(pieces[piece].at[index], rows.at[block - 1, column_of(at, side, turn, low)])
        lanes = turned.shape[2]
        for side in range(2):
            for turn in range(4):
                for level in range(2):
                    piece, index = piece_of(side, turn, THROUGH_AT)
                    source = pieces[piece].at[index, :, pl.ds(level * lanes, lanes)]
                    bring(source, turned.at[column_of(at, side, turn, (at[2] + level) % 2)])
        fetch(0, 0)
        for copy in copies:
            copy.wait()
        for block in range(4):
            here = pl.ds(block * height, height)
            pending = lead[here, :]
            if block:
                before = block * height
                left = rows[block - 1, : before // width].reshape(before, height).T
                pending = pending - triple(left, upper_x[:before, :], lower_x[:before, :])
            solved = triple(inverse_ref[block], *halves(pending))
            upper, lower = halves(solved)
            upper_x[here, :] = upper
            lower_x[here, :] = lower

            @pl.when(x * 2 + high == block)
            def _():
                kept[...] = solved

        count = turned.shape[0]
        left = [turned[i] + pltpu.roll(turned[i + 1], lanes // 2, axis=1) for i in range(0, count, 2)]
        far_ref[...] = triple(jnp.concatenate(left, 1), upper_x[...], lower_x[...])

    @pl.when(step + 1 < pl.num_programs(0))
    def _():
        fetch(step + 1, 1 - slot)

    for number in range(16):
        pltpu.make_async_copy(pieces[0].at[0], panel.at[slot, 0], panel_sems.at[slot, number]).wait()
    left = panel[slot].reshape(known, height).T
    out_ref[0] = rhs_ref[0] - triple(left, upper_x[...], lower_x[...])

    @pl.when(jnp.logical_and(step == 0, x < 2))
    def _():
        out_ref[0] = kept[...]


def late(at, leads, pieces, share, inverses, rhs):
    blocks, height, span = rhs.shape
    width = pieces[0].shape[1]
    lanes = pieces[0].shape[2] // 2
    known = 4 * height
    anywhere = pl.BlockSpec(memory_space=pl.ANY)
    block = pl.BlockSpec((1, height, span), lambda i, s: (i, 0, 0))
    return pl.pallas_call(
        late_kernel,
        out_shape=(
            jax.ShapeDtypeStruct(rhs.shape, F32),
            jax.ShapeDtypeStruct((share, span), F32),
        ),
        grid_spec=pltpu.PrefetchScalarGridSpec(
            num_scalar_prefetch=1,
            grid=(blocks,),
            in_specs=[anywhere] * 14 + [pl.BlockSpec(inverses.shape, lambda i, s: (0, 0, 0)), block],
            out_specs=(block, pl.BlockSpec((share, span), lambda i, s: (0, 0))),
            scratch_shapes=[
                pltpu.VMEM((2, known // width, width, height), F32),
                pltpu.VMEM((known, span), F32),
                pltpu.VMEM((3, known // width, width, height), F32),
                pltpu.VMEM((16, share, lanes), F32),
                pltpu.VMEM((known, span), BF16),
                pltpu.VMEM((known, span), BF16),
                pltpu.VMEM((height, span), F32),
                pltpu.SemaphoreType.DMA((2, 16)),
                pltpu.SemaphoreType.DMA((52,)),
            ],
        ),
        cost_estimate=pl.CostEstimate(
            flops=6 * blocks * height * known * span, bytes_accessed=32 << 20, transcendentals=0
        ),
        name="late",
    )(at, *leads, *pieces, inverses, rhs)


def summed(sums):
    sums = (
        sums[0]
        + lax.ppermute(sums[3], ROWS, X_DOWN)
        + lax.ppermute(sums[1], ROWS, X_UP)
        + lax.ppermute(sums[2], ROWS, X_TWO)
    )
    return sums[0] + lax.ppermute(sums[1], ROWS, HIGH)


def step(right_side, factor, inverses, far_operator):
    row, column = lax.axis_index(ROWS), lax.axis_index(RHS)
    x, high = row // 2, row % 2
    low, y, core = column // 8, column // 2 % 4, column % 2
    at = jnp.stack([x, high, low, y, core]).astype(jnp.int32)
    share = far_operator.shape[0] // 8
    rhs = right_side[:, 0]
    span = rhs.shape[2]
    own = jnp.swapaxes(factor[:, 0], 1, 2)
    far_lines = far_operator.reshape(far_operator.shape[0], -1, 128)

    slab = own[0]
    slab = jnp.stack([slab, lax.ppermute(slab, RHS, LOW)])
    level = lax.ppermute(own, RHS, LOW)
    near = jnp.where(x < 2, slab, lax.ppermute(slab, ROWS, LEAD_OUT))
    pair = lax.ppermute(near, ROWS, X_PAIR)
    near = jnp.stack([near, pair])
    held = jnp.concatenate([near, lax.ppermute(near, ROWS, HIGH)], 0)
    held = held.reshape(8, *own.shape[1:])

    sums = far_part(through_kernel, at, far_lines, own, share, 128)
    through = summed(sums)

    value = pack(at, own, level, held, through, lax.ppermute(through, RHS, LOW))

    from_down = lax.ppermute(value, RHS, Y_UP)
    from_up = lax.ppermute(value, RHS, Y_DOWN)
    pieces = [
        value,
        from_down,
        from_up,
        lax.ppermute(from_down[:HALF], RHS, Y_UP),
        lax.ppermute(from_up[HALF:], RHS, Y_DOWN),
    ]
    pieces += [lax.ppermute(value, RHS, CORE) for value in pieces]

    out = lax.ppermute(rhs[0], ROWS, LEAD_OUT)
    first = jnp.where(x < 2, rhs[0], out)
    second = lax.ppermute(first, ROWS, X_PAIR)
    leads = (first, lax.ppermute(first, ROWS, HIGH), second, lax.ppermute(second, ROWS, HIGH))

    sums = far_part(early_kernel, at, far_lines, rhs, share, span)
    direct = summed(sums)

    solved, rest = late(at, leads, pieces, share, inverses, rhs)
    return solved[:, None], direct + rest


def solution(mesh):
    return jax.shard_map(
        step,
        mesh=mesh,
        in_specs=(
            P(None, "row", None, "rhs"),
            P(None, "row", None, "rhs"),
            P(),
            P(None, None, "row", None),
        ),
        out_specs=(P(None, "row", None, "rhs"), P("row", "rhs")),
        check_vma=False,
    )
```

```python
import jax
import jax.numpy as jnp
from jax import lax
from jax.experimental import pallas as pl
from jax.experimental.pallas import tpu as pltpu
from jax.sharding import PartitionSpec as P


F32 = jnp.float32
BF16 = jnp.bfloat16
ROWS, RHS = "row", "rhs"


def row_pairs(move):
    pairs = []
    for x in range(4):
        for high in range(2):
            target = move(x, high)
            if target is not None:
                pairs.append((x * 2 + high, (target[0] % 4) * 2 + target[1]))
    return pairs


def rhs_pairs(move):
    pairs = []
    for low in range(2):
        for y in range(4):
            for core in range(2):
                to = move(low, y, core)
                pairs.append((low * 8 + y * 2 + core, to[0] * 8 + (to[1] % 4) * 2 + to[2]))
    return pairs


CORE = rhs_pairs(lambda low, y, core: (low, y, 1 - core))
HIGH = row_pairs(lambda x, high: (x, 1 - high))
X_UP = row_pairs(lambda x, high: (x + 1, high))
X_DOWN = row_pairs(lambda x, high: (x - 1, high))
X_TWO = row_pairs(lambda x, high: (x + 2, high))
X_PAIR = row_pairs(lambda x, high: (x ^ 1, high))
LEAD_OUT = row_pairs(lambda x, high: (3 - x, high) if x < 2 else None)
LOW = rhs_pairs(lambda low, y, core: (1 - low, y, core))
Y_UP = rhs_pairs(lambda low, y, core: (low, y + 1, core))
Y_DOWN = rhs_pairs(lambda low, y, core: (low, y - 1, core))


def halves(value):
    upper = value.astype(BF16)
    return upper, (value - upper.astype(F32)).astype(BF16)


def dot(left, right):
    return jnp.dot(left, right, preferred_element_type=F32)


def triple(left, right_upper, right_lower):
    upper, lower = halves(left)
    return dot(
        jnp.concatenate([upper, lower, upper], 1),
        jnp.concatenate([right_upper, right_upper, right_lower], 0),
    )


def triple_lanes(left, right):
    dims = (((1,), (1,)), ((), ()))
    one = lambda a, b: lax.dot_general(a, b, dims, preferred_element_type=F32)
    upper, lower = halves(left)
    right_upper, right_lower = halves(right)
    return one(upper, right_upper) + one(lower, right_upper) + one(upper, right_lower)


def hand_over(at, total, outs):
    share = outs[0].shape[1]
    for ahead, out_ref in enumerate(outs):
        place = ((at[0] + ahead) % 4) * 2
        for side in range(2):
            turn = at[1] if side == 0 else 1 - at[1]
            out_ref[side] = total[pl.ds((place + turn) * share, share), :]


def far_block(far_ref, far, sems):
    step = pl.program_id(0)
    parts = far.shape[0] // pl.num_programs(0)

    def copy(part):
        return pltpu.make_async_copy(far_ref.at[:, part], far.at[part], sems.at[part])

    @pl.when(step == 0)
    def _():
        for part in range(far.shape[0]):
            copy(part).start()

    for part in range(parts):
        copy(step * parts + part).wait()
    return jnp.concatenate([far[step * parts + part] for part in range(parts)], 1)


def through_kernel(at, far_ref, own_ref, *refs):
    outs, (total, far, sems) = refs[:4], refs[4:]
    step = pl.program_id(0)
    x, high, low, y, core = at[0], at[1], at[2], at[3], at[4]
    width = own_ref.shape[1]
    left = far_block(far_ref, far, sems)
    column = low * 8 + y * 2 + core
    owner = jnp.where(x * 2 + high == column // 4, 1.0, 0.0)
    line = lax.broadcasted_iota(jnp.int32, own_ref.shape[1:], 0) + (column % 4) * width
    lane = lax.broadcasted_iota(jnp.int32, own_ref.shape[1:], 1)
    picked = jnp.where(line == lane, -owner, 0.0)
    own = jnp.where(jnp.logical_and(step == 0, x < 2), picked, own_ref[0])
    own = jnp.concatenate([own, jnp.zeros_like(own)], 0)
    through = triple_lanes(left, own)

    @pl.when(step == 0)
    def _():
        total[...] = -through

    @pl.when(step > 0)
    def _():
        total[...] -= through

    @pl.when(step == pl.num_programs(0) - 1)
    def _():
        hand_over(at, total, outs)


def early_kernel(at, far_ref, rhs_ref, *refs):
    outs, (total, far, sems) = refs[:4], refs[4:]
    step = pl.program_id(0)
    left = far_block(far_ref, far, sems)
    left = jnp.where(jnp.logical_and(step == 0, at[0] < 2), 0.0, left)
    direct = triple(left, *halves(rhs_ref[0]))

    @pl.when(step == 0)
    def _():
        total[...] = direct

    @pl.when(step > 0)
    def _():
        total[...] += direct

    @pl.when(step == pl.num_programs(0) - 1)
    def _():
        hand_over(at, total, outs)


def far_part(kernel, at, far_lines, operand, share, lanes):
    blocks, depth, span = operand.shape
    angles, parts, line = far_lines.shape
    shape = (2, share, lanes)
    return pl.pallas_call(
        kernel,
        out_shape=[jax.ShapeDtypeStruct(shape, F32)] * 4,
        grid_spec=pltpu.PrefetchScalarGridSpec(
            num_scalar_prefetch=1,
            grid=(blocks,),
            in_specs=[
                pl.BlockSpec(memory_space=pl.ANY),
                pl.BlockSpec((1, depth, span), lambda i, s: (i, 0, 0)),
            ],
            out_specs=[pl.BlockSpec(shape, lambda i, s: (0, 0, 0))] * 4,
            scratch_shapes=[
                pltpu.VMEM((angles, lanes), F32),
                pltpu.VMEM((parts, angles, line), F32),
                pltpu.SemaphoreType.DMA((parts,)),
            ],
        ),
        cost_estimate=pl.CostEstimate(
            flops=6 * blocks * angles * 256 * lanes, bytes_accessed=12 << 20, transcendentals=0
        ),
    )(at, far_lines, operand)


TURNS = (0, 3, 1, 2)
LEAD_SLICES = ((0, 1), (0, 2), (0, 3), (1, 3))
LEAD_AT = 8
THROUGH_AT = 12
PIECES = 8
CUTS = (4, 7)


def piece_of(side, turn, group, index):
    if turn < 3:
        return side * PIECES + group * 3 + turn, index
    offset = CUTS[0] if group else 0
    if index < CUTS[group]:
        return side * PIECES + 6, offset + index
    return side * PIECES + 7, offset + index - CUTS[group]


def column_of(at, side, turn, low):
    return low * 8 + ((at[3] + TURNS[turn]) % 4) * 2 + (at[4] + side) % 2


def pack_kernel(at, level, held, near, far, out_ref):
    x, high, low = at[0], at[1], at[2]
    near_x = jnp.where(x < 2, x, 3 - x)
    out_ref[:LEAD_AT] = level[...]
    for number, (want_low, block) in enumerate(LEAD_SLICES):
        place = (
            jnp.where(high != block % 2, 4, 0)
            + jnp.where(near_x != block // 2, 2, 0)
            + jnp.where(low != want_low, 1, 0)
        )
        out_ref[LEAD_AT + number] = held[place]
    lanes = near.shape[1]
    out_ref[THROUGH_AT, :, :lanes] = near[...]
    out_ref[THROUGH_AT, :, lanes:] = far[...]


def pack(at, *operands):
    shape = (THROUGH_AT + 1, *operands[0].shape[1:])
    whole = lambda shape: pl.BlockSpec(shape, lambda i, s: (0,) * len(shape))
    return pl.pallas_call(
        pack_kernel,
        out_shape=jax.ShapeDtypeStruct(shape, F32),
        grid_spec=pltpu.PrefetchScalarGridSpec(
            num_scalar_prefetch=1,
            grid=(1,),
            in_specs=[whole(a.shape) for a in operands],
            out_specs=whole(shape),
        ),
        cost_estimate=pl.CostEstimate(flops=0, bytes_accessed=3 << 20, transcendentals=0),
        name="pack",
    )(at, *operands)


def late_kernel(at, *refs):
    leads, refs = refs[:4], refs[4:]
    pieces, refs = refs[: 2 * PIECES], refs[2 * PIECES :]
    inverse_ref, rhs_ref, out_ref, far_ref = refs[:4]
    panel, lead, rows, turned, upper_x, lower_x, kept, panel_sems, sems = refs[4:]
    step = pl.program_id(0)
    slot = lax.rem(step, 2)
    x, high = at[0], at[1]
    height = kept.shape[0]
    known = lead.shape[0]
    width = rows.shape[2]

    def fetch(block, slot):
        for side in range(2):
            for turn in range(4):
                for level in range(2):
                    low = (at[2] + level) % 2
                    into = panel.at[slot, column_of(at, side, turn, low)]
                    sem = panel_sems.at[slot, side * 8 + turn * 2 + level]
                    if turn < 3:
                        piece, _ = piece_of(side, turn, level, 0)
                        pltpu.make_async_copy(pieces[piece].at[block], into, sem).start()
                    else:
                        cut = CUTS[level]
                        piece, offset = piece_of(side, turn, level, 0)

                        @pl.when(block < cut)
                        def _():
                            source = pieces[piece].at[offset + block]
                            pltpu.make_async_copy(source, into, sem).start()

                        @pl.when(block >= cut)
                        def _():
                            source = pieces[piece + 1].at[offset + block - cut]
                            pltpu.make_async_copy(source, into, sem).start()

    @pl.when(step == 0)
    def _():
        copies = []

        def bring(source, into):
            copy = pltpu.make_async_copy(source, into, sems.at[len(copies)])
            copy.start()
            copies.append(copy)

        for pair in range(2):
            near = jnp.where(x < 2, x, 3 - x) if pair == 0 else jnp.where(x < 2, 1 - x, x - 2)
            for side in range(2):
                block = near * 2 + (high if side == 0 else 1 - high)
                bring(leads[pair * 2 + side], lead.at[pl.ds(block * height, height)])
        for side in range(2):
            for turn in range(4):
                for number, (low, block) in enumerate(LEAD_SLICES):
                    piece, index = piece_of(side, turn, 1, LEAD_AT + number)
                    bring(pieces[piece].at[index], rows.at[block - 1, column_of(at, side, turn, low)])
        lanes = turned.shape[2]
        for side in range(2):
            for turn in range(4):
                for level in range(2):
                    piece, index = piece_of(side, turn, 1, THROUGH_AT)
                    source = pieces[piece].at[index, :, pl.ds(level * lanes, lanes)]
                    bring(source, turned.at[column_of(at, side, turn, (at[2] + level) % 2)])
        fetch(0, 0)
        for copy in copies:
            copy.wait()
        for block in range(4):
            here = pl.ds(block * height, height)
            pending = lead[here, :]
            if block:
                before = block * height
                left = rows[block - 1, : before // width].reshape(before, height).T
                pending = pending - triple(left, upper_x[:before, :], lower_x[:before, :])
            solved = triple(inverse_ref[block], *halves(pending))
            upper, lower = halves(solved)
            upper_x[here, :] = upper
            lower_x[here, :] = lower

            @pl.when(x * 2 + high == block)
            def _():
                kept[...] = solved

        count = turned.shape[0]
        left = [turned[i] + pltpu.roll(turned[i + 1], lanes // 2, axis=1) for i in range(0, count, 2)]
        far_ref[...] = triple(jnp.concatenate(left, 1), upper_x[...], lower_x[...])

    @pl.when(step + 1 < pl.num_programs(0))
    def _():
        fetch(step + 1, 1 - slot)

    for number in range(16):
        pltpu.make_async_copy(pieces[0].at[0], panel.at[slot, 0], panel_sems.at[slot, number]).wait()
    left = panel[slot].reshape(known, height).T
    out_ref[0] = rhs_ref[0] - triple(left, upper_x[...], lower_x[...])

    @pl.when(jnp.logical_and(step == 0, x < 2))
    def _():
        out_ref[0] = kept[...]


def late(at, leads, pieces, share, inverses, rhs):
    blocks, height, span = rhs.shape
    width = pieces[0].shape[1]
    lanes = pieces[0].shape[2] // 2
    known = 4 * height
    anywhere = pl.BlockSpec(memory_space=pl.ANY)
    block = pl.BlockSpec((1, height, span), lambda i, s: (i, 0, 0))
    return pl.pallas_call(
        late_kernel,
        out_shape=(
            jax.ShapeDtypeStruct(rhs.shape, F32),
            jax.ShapeDtypeStruct((share, span), F32),
        ),
        grid_spec=pltpu.PrefetchScalarGridSpec(
            num_scalar_prefetch=1,
            grid=(blocks,),
            in_specs=[anywhere] * (4 + 2 * PIECES)
            + [pl.BlockSpec(inverses.shape, lambda i, s: (0, 0, 0)), block],
            out_specs=(block, pl.BlockSpec((share, span), lambda i, s: (0, 0))),
            scratch_shapes=[
                pltpu.VMEM((2, known // width, width, height), F32),
                pltpu.VMEM((known, span), F32),
                pltpu.VMEM((3, known // width, width, height), F32),
                pltpu.VMEM((16, share, lanes), F32),
                pltpu.VMEM((known, span), BF16),
                pltpu.VMEM((known, span), BF16),
                pltpu.VMEM((height, span), F32),
                pltpu.SemaphoreType.DMA((2, 16)),
                pltpu.SemaphoreType.DMA((52,)),
            ],
        ),
        cost_estimate=pl.CostEstimate(
            flops=6 * blocks * height * known * span, bytes_accessed=32 << 20, transcendentals=0
        ),
        name="late",
    )(at, *leads, *pieces, inverses, rhs)


def summed(sums):
    sums = (
        sums[0]
        + lax.ppermute(sums[3], ROWS, X_DOWN)
        + lax.ppermute(sums[1], ROWS, X_UP)
        + lax.ppermute(sums[2], ROWS, X_TWO)
    )
    return sums[0] + lax.ppermute(sums[1], ROWS, HIGH)


def step(right_side, factor, inverses, far_operator):
    row, column = lax.axis_index(ROWS), lax.axis_index(RHS)
    x, high = row // 2, row % 2
    low, y, core = column // 8, column // 2 % 4, column % 2
    at = jnp.stack([x, high, low, y, core]).astype(jnp.int32)
    share = far_operator.shape[0] // 8
    rhs = right_side[:, 0]
    span = rhs.shape[2]
    own = jnp.swapaxes(factor[:, 0], 1, 2)
    height = own.shape[2]
    _, height = own.shape[1:]
    far_lines = far_operator.reshape(far_operator.shape[0], -1, 128)

    slab = own[0]
    slab = jnp.stack([slab, lax.ppermute(slab, RHS, LOW)])
    level = lax.ppermute(own, RHS, LOW)
    near = jnp.where(x < 2, slab, lax.ppermute(slab, ROWS, LEAD_OUT))
    pair = lax.ppermute(near, ROWS, X_PAIR)
    near = jnp.stack([near, pair])
    held = jnp.concatenate([near, lax.ppermute(near, ROWS, HIGH)], 0)
    held = held.reshape(8, *own.shape[1:])

    sums = far_part(through_kernel, at, far_lines, own, share, 128)
    through = summed(sums)

    packed = pack(at, level, held, through, lax.ppermute(through, RHS, LOW))

    pieces = []
    for value in (own, packed):
        pieces += [value, lax.ppermute(value, RHS, Y_UP), lax.ppermute(value, RHS, Y_DOWN)]
    on_up = jnp.concatenate([pieces[1][: CUTS[0]], pieces[4][: CUTS[1]]], 0)
    on_down = jnp.concatenate([pieces[2][CUTS[0] :], pieces[5][CUTS[1] :]], 0)
    pieces += [lax.ppermute(on_up, RHS, Y_UP), lax.ppermute(on_down, RHS, Y_DOWN)]
    pieces += [lax.ppermute(value, RHS, CORE) for value in pieces]

    half = height // 2
    out = [
        lax.ppermute(rhs[0, part * half : (part + 1) * half], ROWS, LEAD_OUT)
        for part in range(2)
    ]
    first = jnp.where(x < 2, rhs[0], jnp.concatenate(out, 0))
    second = lax.ppermute(first, ROWS, X_PAIR)
    leads = (first, lax.ppermute(first, ROWS, HIGH), second, lax.ppermute(second, ROWS, HIGH))

    sums = far_part(early_kernel, at, far_lines, rhs, share, span)
    direct = summed(sums)

    solved, rest = late(at, leads, pieces, share, inverses, rhs)
    return solved[:, None], direct + rest


def solution(mesh):
    return jax.shard_map(
        step,
        mesh=mesh,
        in_specs=(
            P(None, "row", None, "rhs"),
            P(None, "row", None, "rhs"),
            P(),
            P(None, None, "row", None),
        ),
        out_specs=(P(None, "row", None, "rhs"), P("row", "rhs")),
        check_vma=False,
    )
```

```python
import jax
import jax.numpy as jnp
from jax import lax
from jax.experimental import pallas as pl
from jax.experimental.pallas import tpu as pltpu
from jax.sharding import PartitionSpec as P


F32 = jnp.float32
BF16 = jnp.bfloat16
ROWS, RHS = "row", "rhs"


def row_pairs(move):
    pairs = []
    for x in range(4):
        for high in range(2):
            target = move(x, high)
            if target is not None:
                pairs.append((x * 2 + high, (target[0] % 4) * 2 + target[1]))
    return pairs


def rhs_pairs(move):
    pairs = []
    for low in range(2):
        for y in range(4):
            for core in range(2):
                to = move(low, y, core)
                pairs.append((low * 8 + y * 2 + core, to[0] * 8 + (to[1] % 4) * 2 + to[2]))
    return pairs


CORE = rhs_pairs(lambda low, y, core: (low, y, 1 - core))
HIGH = row_pairs(lambda x, high: (x, 1 - high))
X_UP = row_pairs(lambda x, high: (x + 1, high))
X_DOWN = row_pairs(lambda x, high: (x - 1, high))
X_TWO = row_pairs(lambda x, high: (x + 2, high))
X_PAIR = row_pairs(lambda x, high: (x ^ 1, high))
LEAD_OUT = row_pairs(lambda x, high: (3 - x, high) if x < 2 else None)
LOW = rhs_pairs(lambda low, y, core: (1 - low, y, core))
Y_UP = rhs_pairs(lambda low, y, core: (low, y + 1, core))
Y_DOWN = rhs_pairs(lambda low, y, core: (low, y - 1, core))
Y_ONE = rhs_pairs(lambda low, y, core: (low, y ^ 1, core))
Y_TWO = rhs_pairs(lambda low, y, core: (low, y ^ 2, core))


def halves(value):
    upper = value.astype(BF16)
    return upper, (value - upper.astype(F32)).astype(BF16)


def dot(left, right):
    return jnp.dot(left, right, preferred_element_type=F32)


def triple(left, right_upper, right_lower):
    upper, lower = halves(left)
    return dot(
        jnp.concatenate([upper, lower, upper], 1),
        jnp.concatenate([right_upper, right_upper, right_lower], 0),
    )


def triple_lanes(left, right):
    dims = (((1,), (1,)), ((), ()))
    one = lambda a, b: lax.dot_general(a, b, dims, preferred_element_type=F32)
    upper, lower = halves(left)
    right_upper, right_lower = halves(right)
    return one(upper, right_upper) + one(lower, right_upper) + one(upper, right_lower)


def far_block(far_ref, step, angles):
    per = far_ref.shape[0] // angles
    return jnp.concatenate(
        [far_ref[pl.ds(2 * step + part, angles, stride=per), :] for part in range(2)], 1
    )


def hand_over(at, total, mine_ref, other_ref):
    share = mine_ref.shape[1]
    for ahead in range(4):
        place = ((at[0] + ahead) % 4) * 2
        mine_ref[ahead] = total[pl.ds((place + at[1]) * share, share), :]
        other_ref[ahead] = total[pl.ds((place + 1 - at[1]) * share, share), :]


def through_kernel(at, far_ref, own_ref, mine_ref, other_ref, total):
    step = pl.program_id(0)
    x, high, low, y, core = at[0], at[1], at[2], at[3], at[4]
    width = own_ref.shape[1]
    left = far_block(far_ref, step, total.shape[0])
    column = low * 8 + y * 2 + core
    owner = jnp.where(x * 2 + high == column // 4, 1.0, 0.0)
    line = lax.broadcasted_iota(jnp.int32, own_ref.shape[1:], 0) + (column % 4) * width
    lane = lax.broadcasted_iota(jnp.int32, own_ref.shape[1:], 1)
    picked = jnp.where(line == lane, -owner, 0.0)
    own = jnp.where(jnp.logical_and(step == 0, x < 2), picked, own_ref[0])
    own = jnp.concatenate([own, jnp.zeros_like(own)], 0)
    through = triple_lanes(left, own)

    @pl.when(step == 0)
    def _():
        total[...] = -through

    @pl.when(step > 0)
    def _():
        total[...] -= through

    @pl.when(step == pl.num_programs(0) - 1)
    def _():
        hand_over(at, total, mine_ref, other_ref)


def early_kernel(at, far_ref, rhs_ref, *refs):
    outs, total = refs[:4], refs[4]
    step = pl.program_id(0)
    left = far_block(far_ref, step, total.shape[0])
    left = jnp.where(jnp.logical_and(step == 0, at[0] < 2), 0.0, left)
    direct = triple(left, *halves(rhs_ref[0]))

    @pl.when(step == 0)
    def _():
        total[...] = direct

    @pl.when(step > 0)
    def _():
        total[...] += direct

    @pl.when(step == pl.num_programs(0) - 1)
    def _():
        share = outs[0].shape[1]
        for ahead, out_ref in enumerate(outs):
            place = ((at[0] + ahead) % 4) * 2
            for side in range(2):
                turn = at[1] if side == 0 else 1 - at[1]
                out_ref[side] = total[pl.ds((place + turn) * share, share), :]


def far_part(kernel, at, far_lines, operand, share, lanes, joined):
    blocks, depth, span = operand.shape
    angles = 8 * share
    shape = (2, share, lanes) if joined else (4, share, lanes)
    out = [jax.ShapeDtypeStruct(shape, F32)] * (4 if joined else 2)
    whole = pl.BlockSpec(shape, lambda i, s: (0, 0, 0))
    return pl.pallas_call(
        kernel,
        out_shape=out,
        grid_spec=pltpu.PrefetchScalarGridSpec(
            num_scalar_prefetch=1,
            grid=(blocks,),
            in_specs=[
                pl.BlockSpec(far_lines.shape, lambda i, s: (0, 0)),
                pl.BlockSpec((1, depth, span), lambda i, s: (i, 0, 0)),
            ],
            out_specs=[whole] * len(out),
            scratch_shapes=[pltpu.VMEM((angles, lanes), F32)],
        ),
        cost_estimate=pl.CostEstimate(
            flops=6 * blocks * angles * 256 * lanes, bytes_accessed=12 << 20, transcendentals=0
        ),
    )(at, far_lines, operand)


TURNS = (0, 3, 1, 2)
LEAD_SLICES = ((0, 1), (0, 2), (0, 3), (1, 3))
LEAD_AT = 16
HALF = 10


def piece_of(side, turn, index):
    if turn < 3:
        return side * 5 + turn, index
    return side * 5 + 3 + index // HALF, index % HALF


def column_of(at, side, turn, low):
    return low * 8 + ((at[3] + TURNS[turn]) % 4) * 2 + (at[4] + side) % 2


def pack_kernel(at, own, level, held, out_ref):
    x, high, low = at[0], at[1], at[2]
    near_x = jnp.where(x < 2, x, 3 - x)
    out_ref[:8] = own[...]
    out_ref[8:16] = level[...]
    for number, (want_low, block) in enumerate(LEAD_SLICES):
        place = (
            jnp.where(high != block % 2, 4, 0)
            + jnp.where(near_x != block // 2, 2, 0)
            + jnp.where(low != want_low, 1, 0)
        )
        out_ref[LEAD_AT + number] = held[place]


def pack(at, own, level, held):
    shape = (LEAD_AT + len(LEAD_SLICES), *own.shape[1:])
    whole = lambda shape: pl.BlockSpec(shape, lambda i, s: (0, 0, 0))
    return pl.pallas_call(
        pack_kernel,
        out_shape=jax.ShapeDtypeStruct(shape, F32),
        grid_spec=pltpu.PrefetchScalarGridSpec(
            num_scalar_prefetch=1,
            grid=(1,),
            in_specs=[whole(own.shape), whole(level.shape), whole(held.shape)],
            out_specs=whole(shape),
        ),
        cost_estimate=pl.CostEstimate(flops=0, bytes_accessed=3 << 20, transcendentals=0),
        name="pack",
    )(at, own, level, held)


def late_kernel(at, *refs):
    leads, pieces, through, refs = refs[:4], refs[4:14], refs[14:16], refs[16:]
    inverse_ref, rhs_ref, out_ref, far_ref = refs[:4]
    panel, lead, rows, turned, upper_x, lower_x, kept, panel_sems, sems = refs[4:]
    step = pl.program_id(0)
    slot = lax.rem(step, 2)
    x, high = at[0], at[1]
    height = kept.shape[0]
    known = lead.shape[0]
    width = rows.shape[2]

    def fetch(block, slot):
        for side in range(2):
            for turn in range(4):
                for level in range(2):
                    low = (at[2] + level) % 2
                    into = panel.at[slot, column_of(at, side, turn, low)]
                    sem = panel_sems.at[slot, side * 8 + turn * 2 + level]
                    if turn < 3 or level == 0:
                        piece, _ = piece_of(side, turn, 0)
                        source = pieces[piece].at[level * 8 + block]
                        pltpu.make_async_copy(source, into, sem).start()
                    else:
                        piece, cut = piece_of(side, turn, 8)

                        @pl.when(block < HALF - cut)
                        def _():
                            pltpu.make_async_copy(pieces[piece].at[cut + block], into, sem).start()

                        @pl.when(block >= HALF - cut)
                        def _():
                            source = pieces[piece + 1].at[block - (HALF - cut)]
                            pltpu.make_async_copy(source, into, sem).start()

    @pl.when(step == 0)
    def _():
        copies = []

        def bring(source, into):
            copy = pltpu.make_async_copy(source, into, sems.at[len(copies)])
            copy.start()
            copies.append(copy)

        for pair in range(2):
            near = jnp.where(x < 2, x, 3 - x) if pair == 0 else jnp.where(x < 2, 1 - x, x - 2)
            for side in range(2):
                block = near * 2 + (high if side == 0 else 1 - high)
                bring(leads[pair * 2 + side], lead.at[pl.ds(block * height, height)])
        for side in range(2):
            for turn in range(4):
                for number, (low, block) in enumerate(LEAD_SLICES):
                    piece, index = piece_of(side, turn, LEAD_AT + number)
                    bring(pieces[piece].at[index], rows.at[block - 1, column_of(at, side, turn, low)])
        for side in range(2):
            for spot in range(8):
                low = (at[2] + spot % 2) % 2
                column = low * 8 + (at[3] ^ (spot // 2)) * 2 + (at[4] + side) % 2
                bring(through[side].at[spot], turned.at[column])
        fetch(0, 0)
        for copy in copies:
            copy.wait()
        for block in range(4):
            here = pl.ds(block * height, height)
            pending = lead[here, :]
            if block:
                before = block * height
                left = rows[block - 1, : before // width].reshape(before, height).T
                pending = pending - triple(left, upper_x[:before, :], lower_x[:before, :])
            solved = triple(inverse_ref[block], *halves(pending))
            upper, lower = halves(solved)
            upper_x[here, :] = upper
            lower_x[here, :] = lower

            @pl.when(x * 2 + high == block)
            def _():
                kept[...] = solved

        count, _, lanes = turned.shape
        left = [turned[i] + pltpu.roll(turned[i + 1], lanes // 2, axis=1) for i in range(0, count, 2)]
        far_ref[...] = triple(jnp.concatenate(left, 1), upper_x[...], lower_x[...])

    @pl.when(step + 1 < pl.num_programs(0))
    def _():
        fetch(step + 1, 1 - slot)

    for number in range(16):
        pltpu.make_async_copy(pieces[0].at[0], panel.at[slot, 0], panel_sems.at[slot, number]).wait()
    left = panel[slot].reshape(known, height).T
    out_ref[0] = rhs_ref[0] - triple(left, upper_x[...], lower_x[...])

    @pl.when(jnp.logical_and(step == 0, x < 2))
    def _():
        out_ref[0] = kept[...]


def late(at, leads, pieces, through, inverses, rhs):
    blocks, height, span = rhs.shape
    width = pieces[0].shape[1]
    share, lanes = through[0].shape[1:]
    known = 4 * height
    anywhere = pl.BlockSpec(memory_space=pl.ANY)
    block = pl.BlockSpec((1, height, span), lambda i, s: (i, 0, 0))
    return pl.pallas_call(
        late_kernel,
        out_shape=(
            jax.ShapeDtypeStruct(rhs.shape, F32),
            jax.ShapeDtypeStruct((share, span), F32),
        ),
        grid_spec=pltpu.PrefetchScalarGridSpec(
            num_scalar_prefetch=1,
            grid=(blocks,),
            in_specs=[anywhere] * 16 + [pl.BlockSpec(inverses.shape, lambda i, s: (0, 0, 0)), block],
            out_specs=(block, pl.BlockSpec((share, span), lambda i, s: (0, 0))),
            scratch_shapes=[
                pltpu.VMEM((2, known // width, width, height), F32),
                pltpu.VMEM((known, span), F32),
                pltpu.VMEM((3, known // width, width, height), F32),
                pltpu.VMEM((16, share, lanes), F32),
                pltpu.VMEM((known, span), BF16),
                pltpu.VMEM((known, span), BF16),
                pltpu.VMEM((height, span), F32),
                pltpu.SemaphoreType.DMA((2, 16)),
                pltpu.SemaphoreType.DMA((52,)),
            ],
        ),
        cost_estimate=pl.CostEstimate(
            flops=6 * blocks * height * known * span, bytes_accessed=32 << 20, transcendentals=0
        ),
        name="late",
    )(at, *leads, *pieces, *through, inverses, rhs)


def step(right_side, factor, inverses, far_operator):
    row, column = lax.axis_index(ROWS), lax.axis_index(RHS)
    x, high = row // 2, row % 2
    low, y, core = column // 8, column // 2 % 4, column % 2
    at = jnp.stack([x, high, low, y, core]).astype(jnp.int32)
    share = far_operator.shape[0] // 8
    rhs = right_side[:, 0]
    span = rhs.shape[2]
    own = jnp.swapaxes(factor[:, 0], 1, 2)
    far_lines = far_operator.reshape(-1, 128)

    slab = own[0]
    slab = jnp.stack([slab, lax.ppermute(slab, RHS, LOW)])
    level = lax.ppermute(own, RHS, LOW)
    near = jnp.where(x < 2, slab, lax.ppermute(slab, ROWS, LEAD_OUT))
    pair = lax.ppermute(near, ROWS, X_PAIR)
    near = jnp.stack([near, pair])
    held = jnp.concatenate([near, lax.ppermute(near, ROWS, HIGH)], 0)
    value = pack(at, own, level, held.reshape(8, *own.shape[1:]))

    from_down = lax.ppermute(value, RHS, Y_UP)
    from_up = lax.ppermute(value, RHS, Y_DOWN)
    pieces = [
        value,
        from_down,
        from_up,
        lax.ppermute(from_down[:HALF], RHS, Y_UP),
        lax.ppermute(from_up[HALF:], RHS, Y_DOWN),
    ]
    pieces += [lax.ppermute(value, RHS, CORE) for value in pieces]

    out = lax.ppermute(rhs[0], ROWS, LEAD_OUT)
    first = jnp.where(x < 2, rhs[0], out)
    second = lax.ppermute(first, ROWS, X_PAIR)
    leads = (first, lax.ppermute(first, ROWS, HIGH), second, lax.ppermute(second, ROWS, HIGH))

    mine, other = far_part(through_kernel, at, far_lines, own, share, 128, False)
    mine = mine + lax.ppermute(other, ROWS, HIGH)
    through = (
        mine[0]
        + lax.ppermute(mine[3], ROWS, X_DOWN)
        + lax.ppermute(mine[1], ROWS, X_UP)
        + lax.ppermute(mine[2], ROWS, X_TWO)
    )[None]
    for pairs in (LOW, Y_ONE, Y_TWO):
        through = jnp.concatenate([through, lax.ppermute(through, RHS, pairs)], 0)
    through = (through, lax.ppermute(through, RHS, CORE))

    sums = far_part(early_kernel, at, far_lines, rhs, share, span, True)
    sums = (
        sums[0]
        + lax.ppermute(sums[3], ROWS, X_DOWN)
        + lax.ppermute(sums[1], ROWS, X_UP)
        + lax.ppermute(sums[2], ROWS, X_TWO)
    )
    direct = sums[0] + lax.ppermute(sums[1], ROWS, HIGH)

    solved, rest = late(at, leads, pieces, through, inverses, rhs)
    return solved[:, None], direct + rest


def solution(mesh):
    return jax.shard_map(
        step,
        mesh=mesh,
        in_specs=(
            P(None, "row", None, "rhs"),
            P(None, "row", None, "rhs"),
            P(),
            P(None, None, "row", None),
        ),
        out_specs=(P(None, "row", None, "rhs"), P("row", "rhs")),
        check_vma=False,
    )
```

```python
import jax
import jax.numpy as jnp
from jax import lax
from jax.experimental import pallas as pl
from jax.experimental.pallas import tpu as pltpu
from jax.sharding import PartitionSpec as P


F32 = jnp.float32
BF16 = jnp.bfloat16
ROWS, RHS = "row", "rhs"


def row_pairs(move):
    pairs = []
    for x in range(4):
        for high in range(2):
            target = move(x, high)
            if target is not None:
                pairs.append((x * 2 + high, (target[0] % 4) * 2 + target[1]))
    return pairs


def rhs_pairs(move):
    pairs = []
    for low in range(2):
        for y in range(4):
            for core in range(2):
                to = move(low, y, core)
                pairs.append((low * 8 + y * 2 + core, to[0] * 8 + (to[1] % 4) * 2 + to[2]))
    return pairs


CORE = rhs_pairs(lambda low, y, core: (low, y, 1 - core))
HIGH = row_pairs(lambda x, high: (x, 1 - high))
X_UP = row_pairs(lambda x, high: (x + 1, high))
X_DOWN = row_pairs(lambda x, high: (x - 1, high))
X_TWO = row_pairs(lambda x, high: (x + 2, high))
X_PAIR = row_pairs(lambda x, high: (x ^ 1, high))
LEAD_OUT = row_pairs(lambda x, high: (3 - x, high) if x < 2 else None)
LOW = rhs_pairs(lambda low, y, core: (1 - low, y, core))
Y_UP = rhs_pairs(lambda low, y, core: (low, y + 1, core))
Y_DOWN = rhs_pairs(lambda low, y, core: (low, y - 1, core))
Y_ONE = rhs_pairs(lambda low, y, core: (low, y ^ 1, core))
Y_TWO = rhs_pairs(lambda low, y, core: (low, y ^ 2, core))


def halves(value):
    upper = value.astype(BF16)
    return upper, (value - upper.astype(F32)).astype(BF16)


def dot(left, right):
    return jnp.dot(left, right, preferred_element_type=F32)


def triple(left, right_upper, right_lower):
    upper, lower = halves(left)
    return dot(
        jnp.concatenate([upper, lower, upper], 1),
        jnp.concatenate([right_upper, right_upper, right_lower], 0),
    )


def triple_lanes(left, right):
    dims = (((1,), (1,)), ((), ()))
    one = lambda a, b: lax.dot_general(a, b, dims, preferred_element_type=F32)
    upper, lower = halves(left)
    right_upper, right_lower = halves(right)
    return one(upper, right_upper) + one(lower, right_upper) + one(upper, right_lower)


def far_block(far_ref, step, angles):
    per = far_ref.shape[0] // angles
    return jnp.concatenate(
        [far_ref[pl.ds(2 * step + part, angles, stride=per), :] for part in range(2)], 1
    )


def hand_over(at, total, mine_ref, other_ref):
    share = mine_ref.shape[1]
    for ahead in range(4):
        place = ((at[0] + ahead) % 4) * 2
        mine_ref[ahead] = total[pl.ds((place + at[1]) * share, share), :]
        other_ref[ahead] = total[pl.ds((place + 1 - at[1]) * share, share), :]


def through_kernel(at, far_ref, own_ref, mine_ref, other_ref, total):
    step = pl.program_id(0)
    x, high, low, y, core = at[0], at[1], at[2], at[3], at[4]
    width = own_ref.shape[1]
    left = far_block(far_ref, step, total.shape[0])
    column = low * 8 + y * 2 + core
    owner = jnp.where(x * 2 + high == column // 4, 1.0, 0.0)
    line = lax.broadcasted_iota(jnp.int32, own_ref.shape[1:], 0) + (column % 4) * width
    lane = lax.broadcasted_iota(jnp.int32, own_ref.shape[1:], 1)
    picked = jnp.where(line == lane, -owner, 0.0)
    own = jnp.where(jnp.logical_and(step == 0, x < 2), picked, own_ref[0])
    own = jnp.concatenate([own, jnp.zeros_like(own)], 0)
    through = triple_lanes(left, own)

    @pl.when(step == 0)
    def _():
        total[...] = -through

    @pl.when(step > 0)
    def _():
        total[...] -= through

    @pl.when(step == pl.num_programs(0) - 1)
    def _():
        hand_over(at, total, mine_ref, other_ref)


def early_kernel(at, far_ref, rhs_ref, *refs):
    outs, total = refs[:4], refs[4]
    step = pl.program_id(0)
    left = far_block(far_ref, step, total.shape[0])
    left = jnp.where(jnp.logical_and(step == 0, at[0] < 2), 0.0, left)
    direct = triple(left, *halves(rhs_ref[0]))

    @pl.when(step == 0)
    def _():
        total[...] = direct

    @pl.when(step > 0)
    def _():
        total[...] += direct

    @pl.when(step == pl.num_programs(0) - 1)
    def _():
        share = outs[0].shape[1]
        for ahead, out_ref in enumerate(outs):
            place = ((at[0] + ahead) % 4) * 2
            for side in range(2):
                turn = at[1] if side == 0 else 1 - at[1]
                out_ref[side] = total[pl.ds((place + turn) * share, share), :]


def far_part(kernel, at, far_lines, operand, share, lanes, joined):
    blocks, depth, span = operand.shape
    angles = 8 * share
    shape = (2, share, lanes) if joined else (4, share, lanes)
    out = [jax.ShapeDtypeStruct(shape, F32)] * (4 if joined else 2)
    whole = pl.BlockSpec(shape, lambda i, s: (0, 0, 0))
    return pl.pallas_call(
        kernel,
        out_shape=out,
        grid_spec=pltpu.PrefetchScalarGridSpec(
            num_scalar_prefetch=1,
            grid=(blocks,),
            in_specs=[
                pl.BlockSpec(far_lines.shape, lambda i, s: (0, 0)),
                pl.BlockSpec((1, depth, span), lambda i, s: (i, 0, 0)),
            ],
            out_specs=[whole] * len(out),
            scratch_shapes=[pltpu.VMEM((angles, lanes), F32)],
        ),
        cost_estimate=pl.CostEstimate(
            flops=6 * blocks * angles * 256 * lanes, bytes_accessed=12 << 20, transcendentals=0
        ),
    )(at, far_lines, operand)


TURNS = (0, 3, 1, 2)
LEAD_SLICES = ((0, 1), (0, 2), (0, 3), (1, 3))
LEAD_AT = 16
HALF = 10


def piece_of(side, turn, index):
    if turn < 3:
        return side * 5 + turn, index
    return side * 5 + 3 + index // HALF, index % HALF


def column_of(at, side, turn, low):
    return low * 8 + ((at[3] + TURNS[turn]) % 4) * 2 + (at[4] + side) % 2


def pack_kernel(at, own, level, near, pair, far, out_ref):
    x, high, low = at[0], at[1], at[2]
    near_x = jnp.where(x < 2, x, 3 - x)
    out_ref[:8] = own[...]
    out_ref[8:LEAD_AT] = level[...]
    for number, (want_low, block) in enumerate(LEAD_SLICES):
        place = jnp.where(low != want_low, 1, 0)
        same = high == block % 2
        here = near_x == block // 2
        mine = jnp.where(here, near[place], pair[place])
        theirs = far[jnp.where(here, 0, 1), place]
        out_ref[LEAD_AT + number] = jnp.where(same, mine, theirs)


def pack(at, *operands):
    shape = (LEAD_AT + len(LEAD_SLICES), *operands[0].shape[1:])
    inside = pl.BlockSpec(memory_space=pltpu.VMEM)
    return pl.pallas_call(
        pack_kernel,
        out_shape=jax.ShapeDtypeStruct(shape, F32),
        grid_spec=pltpu.PrefetchScalarGridSpec(
            num_scalar_prefetch=1,
            grid=(),
            in_specs=[inside] * len(operands),
            out_specs=inside,
        ),
        compiler_params=pltpu.CompilerParams(vmem_limit_bytes=16 << 20),
        cost_estimate=pl.CostEstimate(flops=0, bytes_accessed=3 << 20, transcendentals=0),
        name="pack",
    )(at, *operands)


def late_kernel(at, *refs):
    leads, pieces, through, refs = refs[:4], refs[4:14], refs[14:16], refs[16:]
    inverse_ref, rhs_ref, out_ref, far_ref = refs[:4]
    panel, lead, rows, turned, upper_x, lower_x, kept, panel_sems, sems = refs[4:]
    step = pl.program_id(0)
    slot = lax.rem(step, 2)
    x, high = at[0], at[1]
    height = kept.shape[0]
    known = lead.shape[0]
    width = rows.shape[2]

    def fetch(block, slot):
        for side in range(2):
            for turn in range(4):
                for level in range(2):
                    low = (at[2] + level) % 2
                    into = panel.at[slot, column_of(at, side, turn, low)]
                    sem = panel_sems.at[slot, side * 8 + turn * 2 + level]
                    if turn < 3 or level == 0:
                        piece, _ = piece_of(side, turn, 0)
                        source = pieces[piece].at[level * 8 + block]
                        pltpu.make_async_copy(source, into, sem).start()
                    else:
                        piece, cut = piece_of(side, turn, 8)

                        @pl.when(block < HALF - cut)
                        def _():
                            pltpu.make_async_copy(pieces[piece].at[cut + block], into, sem).start()

                        @pl.when(block >= HALF - cut)
                        def _():
                            source = pieces[piece + 1].at[block - (HALF - cut)]
                            pltpu.make_async_copy(source, into, sem).start()

    @pl.when(step == 0)
    def _():
        copies = []

        def bring(source, into):
            copy = pltpu.make_async_copy(source, into, sems.at[len(copies)])
            copy.start()
            copies.append(copy)

        for pair in range(2):
            near = jnp.where(x < 2, x, 3 - x) if pair == 0 else jnp.where(x < 2, 1 - x, x - 2)
            for side in range(2):
                block = near * 2 + (high if side == 0 else 1 - high)
                bring(leads[pair * 2 + side], lead.at[pl.ds(block * height, height)])
        for side in range(2):
            for turn in range(4):
                for number, (low, block) in enumerate(LEAD_SLICES):
                    piece, index = piece_of(side, turn, LEAD_AT + number)
                    bring(pieces[piece].at[index], rows.at[block - 1, column_of(at, side, turn, low)])
        for side in range(2):
            for spot in range(8):
                low = (at[2] + spot % 2) % 2
                column = low * 8 + (at[3] ^ (spot // 2)) * 2 + (at[4] + side) % 2
                bring(through[side].at[spot], turned.at[column])
        fetch(0, 0)
        for copy in copies:
            copy.wait()
        for block in range(4):
            here = pl.ds(block * height, height)
            pending = lead[here, :]
            if block:
                before = block * height
                left = rows[block - 1, : before // width].reshape(before, height).T
                pending = pending - triple(left, upper_x[:before, :], lower_x[:before, :])
            solved = triple(inverse_ref[block], *halves(pending))
            upper, lower = halves(solved)
            upper_x[here, :] = upper
            lower_x[here, :] = lower

            @pl.when(x * 2 + high == block)
            def _():
                kept[...] = solved

        count, _, lanes = turned.shape
        left = [turned[i] + pltpu.roll(turned[i + 1], lanes // 2, axis=1) for i in range(0, count, 2)]
        far_ref[...] = triple(jnp.concatenate(left, 1), upper_x[...], lower_x[...])

    @pl.when(step + 1 < pl.num_programs(0))
    def _():
        fetch(step + 1, 1 - slot)

    for number in range(16):
        pltpu.make_async_copy(pieces[0].at[0], panel.at[slot, 0], panel_sems.at[slot, number]).wait()
    left = panel[slot].reshape(known, height).T
    out_ref[0] = rhs_ref[0] - triple(left, upper_x[...], lower_x[...])

    @pl.when(jnp.logical_and(step == 0, x < 2))
    def _():
        out_ref[0] = kept[...]


def late(at, leads, pieces, through, inverses, rhs):
    blocks, height, span = rhs.shape
    width = pieces[0].shape[1]
    share, lanes = through[0].shape[1:]
    known = 4 * height
    anywhere = pl.BlockSpec(memory_space=pl.ANY)
    block = pl.BlockSpec((1, height, span), lambda i, s: (i, 0, 0))
    return pl.pallas_call(
        late_kernel,
        out_shape=(
            jax.ShapeDtypeStruct(rhs.shape, F32),
            jax.ShapeDtypeStruct((share, span), F32),
        ),
        grid_spec=pltpu.PrefetchScalarGridSpec(
            num_scalar_prefetch=1,
            grid=(blocks,),
            in_specs=[anywhere] * 16 + [pl.BlockSpec(inverses.shape, lambda i, s: (0, 0, 0)), block],
            out_specs=(block, pl.BlockSpec((share, span), lambda i, s: (0, 0))),
            scratch_shapes=[
                pltpu.VMEM((2, known // width, width, height), F32),
                pltpu.VMEM((known, span), F32),
                pltpu.VMEM((3, known // width, width, height), F32),
                pltpu.VMEM((16, share, lanes), F32),
                pltpu.VMEM((known, span), BF16),
                pltpu.VMEM((known, span), BF16),
                pltpu.VMEM((height, span), F32),
                pltpu.SemaphoreType.DMA((2, 16)),
                pltpu.SemaphoreType.DMA((52,)),
            ],
        ),
        cost_estimate=pl.CostEstimate(
            flops=6 * blocks * height * known * span, bytes_accessed=32 << 20, transcendentals=0
        ),
        name="late",
    )(at, *leads, *pieces, *through, inverses, rhs)


def step(right_side, factor, inverses, far_operator):
    row, column = lax.axis_index(ROWS), lax.axis_index(RHS)
    x, high = row // 2, row % 2
    low, y, core = column // 8, column // 2 % 4, column % 2
    at = jnp.stack([x, high, low, y, core]).astype(jnp.int32)
    share = far_operator.shape[0] // 8
    rhs = right_side[:, 0]
    span = rhs.shape[2]
    own = jnp.swapaxes(factor[:, 0], 1, 2)
    far_lines = far_operator.reshape(-1, 128)

    slab = own[0]
    slab = jnp.stack([slab, lax.ppermute(slab, RHS, LOW)])
    level = lax.ppermute(own, RHS, LOW)
    near = jnp.where(x < 2, slab, lax.ppermute(slab, ROWS, LEAD_OUT))
    pair = lax.ppermute(near, ROWS, X_PAIR)
    far = lax.ppermute(jnp.stack([near, pair]), ROWS, HIGH)
    value = pack(at, own, level, near, pair, far)

    from_down = lax.ppermute(value, RHS, Y_UP)
    from_up = lax.ppermute(value, RHS, Y_DOWN)
    pieces = [
        value,
        from_down,
        from_up,
        lax.ppermute(from_down[:HALF], RHS, Y_UP),
        lax.ppermute(from_up[HALF:], RHS, Y_DOWN),
    ]
    pieces += [lax.ppermute(value, RHS, CORE) for value in pieces]

    out = lax.ppermute(rhs[0], ROWS, LEAD_OUT)
    first = jnp.where(x < 2, rhs[0], out)
    second = lax.ppermute(first, ROWS, X_PAIR)
    leads = (first, lax.ppermute(first, ROWS, HIGH), second, lax.ppermute(second, ROWS, HIGH))

    mine, other = far_part(through_kernel, at, far_lines, own, share, 128, False)
    mine = mine + lax.ppermute(other, ROWS, HIGH)
    through = (
        mine[0]
        + lax.ppermute(mine[3], ROWS, X_DOWN)
        + lax.ppermute(mine[1], ROWS, X_UP)
        + lax.ppermute(mine[2], ROWS, X_TWO)
    )[None]
    for pairs in (LOW, Y_ONE, Y_TWO):
        through = jnp.concatenate([through, lax.ppermute(through, RHS, pairs)], 0)
    through = (through, lax.ppermute(through, RHS, CORE))

    sums = far_part(early_kernel, at, far_lines, rhs, share, span, True)
    sums = (
        sums[0]
        + lax.ppermute(sums[3], ROWS, X_DOWN)
        + lax.ppermute(sums[1], ROWS, X_UP)
        + lax.ppermute(sums[2], ROWS, X_TWO)
    )
    direct = sums[0] + lax.ppermute(sums[1], ROWS, HIGH)

    solved, rest = late(at, leads, pieces, through, inverses, rhs)
    return solved[:, None], direct + rest


def solution(mesh):
    return jax.shard_map(
        step,
        mesh=mesh,
        in_specs=(
            P(None, "row", None, "rhs"),
            P(None, "row", None, "rhs"),
            P(),
            P(None, None, "row", None),
        ),
        out_specs=(P(None, "row", None, "rhs"), P("row", "rhs")),
        check_vma=False,
    )
```

```python
import jax
import jax.numpy as jnp
from jax import lax
from jax.experimental import pallas as pl
from jax.experimental.pallas import tpu as pltpu
from jax.sharding import PartitionSpec as P


F32 = jnp.float32
BF16 = jnp.bfloat16
ROWS, RHS = "row", "rhs"


def row_pairs(move):
    pairs = []
    for x in range(4):
        for high in range(2):
            target = move(x, high)
            if target is not None:
                pairs.append((x * 2 + high, (target[0] % 4) * 2 + target[1]))
    return pairs


def rhs_pairs(move):
    pairs = []
    for low in range(2):
        for y in range(4):
            for core in range(2):
                to = move(low, y, core)
                pairs.append((low * 8 + y * 2 + core, to[0] * 8 + (to[1] % 4) * 2 + to[2]))
    return pairs


CORE = rhs_pairs(lambda low, y, core: (low, y, 1 - core))
HIGH = row_pairs(lambda x, high: (x, 1 - high))
X_UP = row_pairs(lambda x, high: (x + 1, high))
X_DOWN = row_pairs(lambda x, high: (x - 1, high))
X_TWO = row_pairs(lambda x, high: (x + 2, high))
X_PAIR = row_pairs(lambda x, high: (x ^ 1, high))
LEAD_OUT = row_pairs(lambda x, high: (3 - x, high) if x < 2 else None)
LOW = rhs_pairs(lambda low, y, core: (1 - low, y, core))
Y_UP = rhs_pairs(lambda low, y, core: (low, y + 1, core))
Y_DOWN = rhs_pairs(lambda low, y, core: (low, y - 1, core))
Y_ONE = rhs_pairs(lambda low, y, core: (low, y ^ 1, core))
Y_TWO = rhs_pairs(lambda low, y, core: (low, y ^ 2, core))


def halves(value):
    upper = value.astype(BF16)
    return upper, (value - upper.astype(F32)).astype(BF16)


def dot(left, right):
    return jnp.dot(left, right, preferred_element_type=F32)


def triple(left, right_upper, right_lower):
    upper, lower = halves(left)
    return dot(
        jnp.concatenate([upper, lower, upper], 1),
        jnp.concatenate([right_upper, right_upper, right_lower], 0),
    )


def triple_lanes(left, right):
    dims = (((1,), (1,)), ((), ()))
    one = lambda a, b: lax.dot_general(a, b, dims, preferred_element_type=F32)
    upper, lower = halves(left)
    right_upper, right_lower = halves(right)
    return one(upper, right_upper) + one(lower, right_upper) + one(upper, right_lower)


def far_block(far_ref, step, angles):
    per = far_ref.shape[0] // angles
    return jnp.concatenate(
        [far_ref[pl.ds(2 * step + part, angles, stride=per), :] for part in range(2)], 1
    )


def hand_over(at, total, mine_ref, other_ref):
    share = mine_ref.shape[1]
    for ahead in range(4):
        place = ((at[0] + ahead) % 4) * 2
        mine_ref[ahead] = total[pl.ds((place + at[1]) * share, share), :]
        other_ref[ahead] = total[pl.ds((place + 1 - at[1]) * share, share), :]


def through_kernel(at, far_ref, own_ref, mine_ref, other_ref, total):
    step = pl.program_id(0)
    x, high, low, y, core = at[0], at[1], at[2], at[3], at[4]
    count, width = own_ref.shape[:2]
    column = low * 8 + y * 2 + core
    owner = jnp.where(x * 2 + high == column // 4, 1.0, 0.0)
    line = lax.broadcasted_iota(jnp.int32, own_ref.shape[1:], 0) + (column % 4) * width
    lane = lax.broadcasted_iota(jnp.int32, own_ref.shape[1:], 1)
    picked = jnp.where(line == lane, -owner, 0.0)
    leads = jnp.logical_and(step == 0, x < 2)
    through = 0.0
    for part in range(count):
        own = own_ref[part]
        if part == 0:
            own = jnp.where(leads, picked, own)
        own = jnp.concatenate([own, jnp.zeros_like(own)], 0)
        left = far_block(far_ref, step * count + part, total.shape[0])
        through = through + triple_lanes(left, own)

    @pl.when(step == 0)
    def _():
        total[...] = -through

    @pl.when(step > 0)
    def _():
        total[...] -= through

    @pl.when(step == pl.num_programs(0) - 1)
    def _():
        hand_over(at, total, mine_ref, other_ref)


def early_kernel(at, far_ref, rhs_ref, *refs):
    outs, total = refs[:4], refs[4]
    step = pl.program_id(0)
    count, height, span = rhs_ref.shape
    lefts = [far_block(far_ref, step * count + part, total.shape[0]) for part in range(count)]
    lefts[0] = jnp.where(jnp.logical_and(step == 0, at[0] < 2), 0.0, lefts[0])
    right = rhs_ref[...].reshape(count * height, span)
    direct = triple(jnp.concatenate(lefts, 1), *halves(right))

    @pl.when(step == 0)
    def _():
        total[...] = direct

    @pl.when(step > 0)
    def _():
        total[...] += direct

    @pl.when(step == pl.num_programs(0) - 1)
    def _():
        share = outs[0].shape[1]
        for ahead, out_ref in enumerate(outs):
            place = ((at[0] + ahead) % 4) * 2
            for side in range(2):
                turn = at[1] if side == 0 else 1 - at[1]
                out_ref[side] = total[pl.ds((place + turn) * share, share), :]


def far_part(kernel, at, far_lines, operand, share, lanes, joined):
    blocks, depth, span = operand.shape
    count = 2 if joined else 4
    angles = 8 * share
    shape = (2, share, lanes) if joined else (4, share, lanes)
    out = [jax.ShapeDtypeStruct(shape, F32)] * (4 if joined else 2)
    whole = pl.BlockSpec(shape, lambda i, s: (0, 0, 0))
    return pl.pallas_call(
        kernel,
        out_shape=out,
        grid_spec=pltpu.PrefetchScalarGridSpec(
            num_scalar_prefetch=1,
            grid=(blocks // count,),
            in_specs=[
                pl.BlockSpec(far_lines.shape, lambda i, s: (0, 0)),
                pl.BlockSpec((count, depth, span), lambda i, s: (i, 0, 0)),
            ],
            out_specs=[whole] * len(out),
            scratch_shapes=[pltpu.VMEM((angles, lanes), F32)],
        ),
        cost_estimate=pl.CostEstimate(
            flops=6 * blocks * angles * 256 * lanes, bytes_accessed=12 << 20, transcendentals=0
        ),
    )(at, far_lines, operand)


TURNS = (0, 3, 1, 2)
LEAD_SLICES = ((0, 1), (0, 2), (0, 3), (1, 3))
LEAD_AT = 16
HALF = 10


def piece_of(side, turn, index):
    if turn < 3:
        return side * 5 + turn, index
    return side * 5 + 3 + index // HALF, index % HALF


def column_of(at, side, turn, low):
    return low * 8 + ((at[3] + TURNS[turn]) % 4) * 2 + (at[4] + side) % 2


def pack_kernel(at, own, level, near, pair, far, out_ref):
    x, high, low = at[0], at[1], at[2]
    near_x = jnp.where(x < 2, x, 3 - x)
    out_ref[:8] = own[...]
    out_ref[8:LEAD_AT] = level[...]
    for number, (want_low, block) in enumerate(LEAD_SLICES):
        place = jnp.where(low != want_low, 1, 0)
        same = high == block % 2
        here = near_x == block // 2
        mine = jnp.where(here, near[place], pair[place])
        theirs = far[jnp.where(here, 0, 1), place]
        out_ref[LEAD_AT + number] = jnp.where(same, mine, theirs)


def pack(at, *operands):
    shape = (LEAD_AT + len(LEAD_SLICES), *operands[0].shape[1:])
    inside = pl.BlockSpec(memory_space=pltpu.VMEM)
    return pl.pallas_call(
        pack_kernel,
        out_shape=jax.ShapeDtypeStruct(shape, F32),
        grid_spec=pltpu.PrefetchScalarGridSpec(
            num_scalar_prefetch=1,
            grid=(),
            in_specs=[inside] * len(operands),
            out_specs=inside,
        ),
        compiler_params=pltpu.CompilerParams(vmem_limit_bytes=16 << 20),
        cost_estimate=pl.CostEstimate(flops=0, bytes_accessed=3 << 20, transcendentals=0),
        name="pack",
    )(at, *operands)


def late_kernel(at, *refs):
    leads, pieces, through, refs = refs[:4], refs[4:14], refs[14:16], refs[16:]
    inverse_ref, rhs_ref, out_ref, far_ref = refs[:4]
    panel, lead, rows, turned, upper_x, lower_x, kept, panel_sems, sems = refs[4:]
    step = pl.program_id(0)
    slot = lax.rem(step, 2)
    x, high = at[0], at[1]
    height = kept.shape[0]
    known = lead.shape[0]
    width = rows.shape[2]

    def fetch(block, slot):
        for side in range(2):
            for turn in range(4):
                for level in range(2):
                    low = (at[2] + level) % 2
                    into = panel.at[slot, column_of(at, side, turn, low)]
                    sem = panel_sems.at[slot, side * 8 + turn * 2 + level]
                    if turn < 3 or level == 0:
                        piece, _ = piece_of(side, turn, 0)
                        source = pieces[piece].at[level * 8 + block]
                        pltpu.make_async_copy(source, into, sem).start()
                    else:
                        piece, cut = piece_of(side, turn, 8)

                        @pl.when(block < HALF - cut)
                        def _():
                            pltpu.make_async_copy(pieces[piece].at[cut + block], into, sem).start()

                        @pl.when(block >= HALF - cut)
                        def _():
                            source = pieces[piece + 1].at[block - (HALF - cut)]
                            pltpu.make_async_copy(source, into, sem).start()

    @pl.when(step == 0)
    def _():
        copies = []

        def bring(source, into):
            copy = pltpu.make_async_copy(source, into, sems.at[len(copies)])
            copy.start()
            copies.append(copy)

        for pair in range(2):
            near = jnp.where(x < 2, x, 3 - x) if pair == 0 else jnp.where(x < 2, 1 - x, x - 2)
            for side in range(2):
                block = near * 2 + (high if side == 0 else 1 - high)
                bring(leads[pair * 2 + side], lead.at[pl.ds(block * height, height)])
        for side in range(2):
            for turn in range(4):
                for number, (low, block) in enumerate(LEAD_SLICES):
                    piece, index = piece_of(side, turn, LEAD_AT + number)
                    bring(pieces[piece].at[index], rows.at[block - 1, column_of(at, side, turn, low)])
        for side in range(2):
            for spot in range(8):
                low = (at[2] + spot % 2) % 2
                column = low * 8 + (at[3] ^ (spot // 2)) * 2 + (at[4] + side) % 2
                bring(through[side].at[spot], turned.at[column])
        fetch(0, 0)
        for copy in copies:
            copy.wait()
        for block in range(4):
            here = pl.ds(block * height, height)
            pending = lead[here, :]
            if block:
                before = block * height
                left = rows[block - 1, : before // width].reshape(before, height).T
                pending = pending - triple(left, upper_x[:before, :], lower_x[:before, :])
            solved = triple(inverse_ref[block], *halves(pending))
            upper, lower = halves(solved)
            upper_x[here, :] = upper
            lower_x[here, :] = lower

            @pl.when(x * 2 + high == block)
            def _():
                kept[...] = solved

        count, _, lanes = turned.shape
        left = [turned[i] + pltpu.roll(turned[i + 1], lanes // 2, axis=1) for i in range(0, count, 2)]
        far_ref[...] = triple(jnp.concatenate(left, 1), upper_x[...], lower_x[...])

    @pl.when(step + 1 < pl.num_programs(0))
    def _():
        fetch(step + 1, 1 - slot)

    for number in range(16):
        pltpu.make_async_copy(pieces[0].at[0], panel.at[slot, 0], panel_sems.at[slot, number]).wait()
    left = panel[slot].reshape(known, height).T
    out_ref[0] = rhs_ref[0] - triple(left, upper_x[...], lower_x[...])

    @pl.when(jnp.logical_and(step == 0, x < 2))
    def _():
        out_ref[0] = kept[...]


def late(at, leads, pieces, through, inverses, rhs):
    blocks, height, span = rhs.shape
    width = pieces[0].shape[1]
    share, lanes = through[0].shape[1:]
    known = 4 * height
    anywhere = pl.BlockSpec(memory_space=pl.ANY)
    block = pl.BlockSpec((1, height, span), lambda i, s: (i, 0, 0))
    return pl.pallas_call(
        late_kernel,
        out_shape=(
            jax.ShapeDtypeStruct(rhs.shape, F32),
            jax.ShapeDtypeStruct((share, span), F32),
        ),
        grid_spec=pltpu.PrefetchScalarGridSpec(
            num_scalar_prefetch=1,
            grid=(blocks,),
            in_specs=[anywhere] * 16 + [pl.BlockSpec(inverses.shape, lambda i, s: (0, 0, 0)), block],
            out_specs=(block, pl.BlockSpec((share, span), lambda i, s: (0, 0))),
            scratch_shapes=[
                pltpu.VMEM((2, known // width, width, height), F32),
                pltpu.VMEM((known, span), F32),
                pltpu.VMEM((3, known // width, width, height), F32),
                pltpu.VMEM((16, share, lanes), F32),
                pltpu.VMEM((known, span), BF16),
                pltpu.VMEM((known, span), BF16),
                pltpu.VMEM((height, span), F32),
                pltpu.SemaphoreType.DMA((2, 16)),
                pltpu.SemaphoreType.DMA((52,)),
            ],
        ),
        cost_estimate=pl.CostEstimate(
            flops=6 * blocks * height * known * span, bytes_accessed=32 << 20, transcendentals=0
        ),
        name="late",
    )(at, *leads, *pieces, *through, inverses, rhs)


def step(right_side, factor, inverses, far_operator):
    row, column = lax.axis_index(ROWS), lax.axis_index(RHS)
    x, high = row // 2, row % 2
    low, y, core = column // 8, column // 2 % 4, column % 2
    at = jnp.stack([x, high, low, y, core]).astype(jnp.int32)
    share = far_operator.shape[0] // 8
    rhs = right_side[:, 0]
    span = rhs.shape[2]
    own = jnp.swapaxes(factor[:, 0], 1, 2)
    far_lines = far_operator.reshape(-1, 128)

    slab = own[0]
    slab = jnp.stack([slab, lax.ppermute(slab, RHS, LOW)])
    level = lax.ppermute(own, RHS, LOW)
    near = jnp.where(x < 2, slab, lax.ppermute(slab, ROWS, LEAD_OUT))
    pair = lax.ppermute(near, ROWS, X_PAIR)
    far = lax.ppermute(jnp.stack([near, pair]), ROWS, HIGH)
    value = pack(at, own, level, near, pair, far)

    from_down = lax.ppermute(value, RHS, Y_UP)
    from_up = lax.ppermute(value, RHS, Y_DOWN)
    pieces = [
        value,
        from_down,
        from_up,
        lax.ppermute(from_down[:HALF], RHS, Y_UP),
        lax.ppermute(from_up[HALF:], RHS, Y_DOWN),
    ]
    pieces += [lax.ppermute(value, RHS, CORE) for value in pieces]

    out = lax.ppermute(rhs[0], ROWS, LEAD_OUT)
    first = jnp.where(x < 2, rhs[0], out)
    second = lax.ppermute(first, ROWS, X_PAIR)
    leads = (first, lax.ppermute(first, ROWS, HIGH), second, lax.ppermute(second, ROWS, HIGH))

    mine, other = far_part(through_kernel, at, far_lines, own, share, 128, False)
    mine = mine + lax.ppermute(other, ROWS, HIGH)
    through = (
        mine[0]
        + lax.ppermute(mine[3], ROWS, X_DOWN)
        + lax.ppermute(mine[1], ROWS, X_UP)
        + lax.ppermute(mine[2], ROWS, X_TWO)
    )[None]
    for pairs in (LOW, Y_ONE, Y_TWO):
        through = jnp.concatenate([through, lax.ppermute(through, RHS, pairs)], 0)
    through = (through, lax.ppermute(through, RHS, CORE))

    sums = far_part(early_kernel, at, far_lines, rhs, share, span, True)
    sums = (
        sums[0]
        + lax.ppermute(sums[3], ROWS, X_DOWN)
        + lax.ppermute(sums[1], ROWS, X_UP)
        + lax.ppermute(sums[2], ROWS, X_TWO)
    )
    direct = sums[0] + lax.ppermute(sums[1], ROWS, HIGH)

    solved, rest = late(at, leads, pieces, through, inverses, rhs)
    return solved[:, None], direct + rest


def solution(mesh):
    return jax.shard_map(
        step,
        mesh=mesh,
        in_specs=(
            P(None, "row", None, "rhs"),
            P(None, "row", None, "rhs"),
            P(),
            P(None, None, "row", None),
        ),
        out_specs=(P(None, "row", None, "rhs"), P("row", "rhs")),
        check_vma=False,
    )
```
